128 devices in a mesh: rec: 4 (over z), tm: 32 (over x, y, core).
Axes of the slice: x: 4, y: 4, z: 4, core: 2. Of those that a mesh axis runs over, the one named last changes fastest.
Arguments:
- mel_frames: bfloat16 [4, 65536, 80], P('rec', 'tm'), may hold values from -6 to 6
- lengths: int32 [4, 4], P('rec'), may hold values from 1 to 32768, 65536 in all within a row
- w_first: float32 [3, 3, 256], replicated, may hold values from -2 to 2
- w_second: bfloat16 [2304, 256], P(('rec', 'tm')), may hold values from -0.125 to 0.125
- w_proj: bfloat16 [5120, 1024], P(('rec', 'tm')), may hold values from -0.078125 to 0.078125
- gain_attn: float32 [1024], replicated, may hold values from 0.5 to 1.5
- w_qkv: bfloat16 [1024, 3072], P(('rec', 'tm')), may hold values from -2 to 2
- w_out: bfloat16 [1024, 1024], P(('rec', 'tm')), may hold values from -0.1875 to 0.1875
- gain_conv: float32 [1024], replicated, may hold values from 0.5 to 1.5
- w_point_in: bfloat16 [1024, 2048], P(('rec', 'tm')), may hold values from -0.1875 to 0.1875
- w_depth: float32 [9, 1024], replicated, may hold values from -6 to 6
- w_point_out: bfloat16 [1024, 1024], P(('rec', 'tm')), may hold values from -0.375 to 0.375
- gain_out: float32 [1024], replicated, may hold values from 0.5 to 1.5
Outputs:
- encoded: bfloat16 [4, 16384, 1024], P('rec', 'tm')
The draws below stay inside these ranges and needn't reach their ends.
Inputs may be any that keep to these rules, and one draw needn't show every extreme that they name: Each group's 4 lengths sum to 65536, and the largest of them is 32768.
All inputs are finite; a program needn't handle non-finite values.
Results may differ from the reference program's by a relative error of at most 0.024.
The reference program's roundings to bfloat16 on the way count: a program that leaves them out, or rounds other values in their place, can miss the bound.
Values may be sent and summed in bfloat16 or wider, within the bound.
A program may use at most 128 MiB of HBM per device.

```python
import math
import jax
import jax.numpy as jnp
import numpy as np
from jax import lax

MEL_BINS = 80
CHANNELS = 256
WIDTH = 1024
HEADS = 8
KERNEL = 9
WINDOW = 128
REC_GROUP = 4
CONV_BLOCK = 64
HEAD_DIM = 128
TOK_DEV = 512
FREQ_QUARTER = 20
FRAMES = 65536
GROUPS = 4


def draw_w_qkv(key, part):
    base_key = jax.random.fold_in(key, 0)
    return (jnp.clip(jax.random.normal(base_key, (WIDTH, 3 * WIDTH), jnp.float32), -6.0, 6.0) / math.sqrt(WIDTH)).astype(jnp.bfloat16)


def levels(key, dims, pieces, low, largest):
    loudness = 1.0
    for axis_at, parts in pieces:
        heights = jax.random.uniform(jax.random.fold_in(jax.random.fold_in(key, 6), axis_at), (parts,), jnp.float32, low / len(pieces), largest / len(pieces))
        loudness = loudness * jnp.repeat(jnp.exp(heights), dims[axis_at] // parts).reshape((-1,) + (1,) * (len(dims) - 1 - axis_at))
    return loudness


def profile(number_of, total, most, slope):
    loads = [(1 << 20) // math.isqrt(grade ** slope) + 1 for grade in range(2, number_of + 1)]
    rest, counts = total - most - (number_of - 1), [1] * (number_of - 1)
    while rest > 0:
        movable = [i for i in range(number_of - 1) if counts[i] < most]
        whole, left = sum([loads[i] for i in movable]), rest
        for i in movable:
            extra = min(most - counts[i], max(1, left * loads[i] // whole), rest)
            counts[i] = counts[i] + extra
            rest = rest - extra
    return np.array([most] + counts)


def ragged(key, count, total, bound, slope):
    if count == 2:
        one = jax.random.randint(key, (), max(1, total - bound), min(bound, total - 1) + 1)
        return jnp.stack([one, total - one])
    sizes = jnp.asarray(profile(count, total, bound, slope), jnp.int32)
    couples = (count - 1) // 2
    giver, receiver = sizes[1:1 + 2 * couples:2], sizes[2:2 + 2 * couples:2]
    room = jnp.minimum(giver - 1, bound - receiver)
    moved = jax.random.randint(jax.random.fold_in(key, 1), (couples,), 0, 1 << 20) % (room + 1)
    sizes = sizes.at[1:1 + 2 * couples:2].set(giver - moved).at[2:2 + 2 * couples:2].set(receiver + moved)
    return sizes[jax.random.permutation(jax.random.fold_in(key, 2), count)]


def noise(stream_key, shape, scale, most, pieces=(), held_as=jnp.bfloat16):
    result = scale * jax.random.normal(stream_key, shape, jnp.float32)
    if pieces:
        result = result * levels(stream_key, shape, pieces, -0.22, 0.18)
    return jnp.clip(result, -most, most).astype(held_as)


def setup_inputs(seed: int = 0) -> dict:
    key_of = jax.random.split(jax.random.key(seed), 14)
    mel_frames = noise(key_of[0], (GROUPS, FRAMES, MEL_BINS), 1.0, 6.0, ((0, 4), (1, 32)))
    lengths = jax.vmap(lambda own: ragged(own, REC_GROUP, FRAMES, FRAMES // 2, 2))(jax.random.split(key_of[1], GROUPS)).reshape((GROUPS, REC_GROUP)).astype(jnp.int32)
    w_first = noise(key_of[2], (3, 3, CHANNELS), 9 ** -0.5, 2.0, (), jnp.float32)
    w_second = noise(key_of[3], (9 * CHANNELS, CHANNELS), (9 * CHANNELS) ** -0.5, 0.125, ((0, 128),))
    w_proj = noise(key_of[4], (FREQ_QUARTER * CHANNELS, WIDTH), (FREQ_QUARTER * CHANNELS) ** -0.5, 0.078125, ((0, 128),))
    gain_attn = jnp.clip(1.0 + 0.1 * jax.random.normal(key_of[5], (WIDTH,), jnp.float32), 0.5, 1.5)
    w_qkv = draw_w_qkv(jax.random.fold_in(key_of[13], 71), 0)
    w_out = noise(key_of[7], (WIDTH, WIDTH), WIDTH ** -0.5, 0.1875, ((0, 128),))
    gain_conv = jnp.clip(1.0 + 0.1 * jax.random.normal(key_of[8], (WIDTH,), jnp.float32), 0.5, 1.5)
    w_point_in = noise(key_of[9], (WIDTH, 2 * WIDTH), WIDTH ** -0.5, 0.1875, ((0, 128),))
    w_depth = noise(key_of[10], (KERNEL, WIDTH), 1 ** -0.5, 6.0, (), jnp.float32)
    w_point_out = noise(key_of[11], (WIDTH, WIDTH), (WIDTH // 4) ** -0.5, 0.375, ((0, 128),))
    gain_out = jnp.clip(1.0 + 0.1 * jax.random.normal(key_of[12], (WIDTH,), jnp.float32), 0.5, 1.5)
    return dict(mel_frames=mel_frames, lengths=lengths, w_first=w_first, w_second=w_second, w_proj=w_proj, gain_attn=gain_attn, w_qkv=w_qkv, w_out=w_out, gain_conv=gain_conv, w_point_in=w_point_in, w_depth=w_depth, w_point_out=w_point_out, gain_out=gain_out)


NORM_EPSILON = 1e-05

def layer_norm(values, gain):
    row_mean = lax.optimization_barrier(jnp.mean(values, axis=-1, keepdims=True))
    centred = values - row_mean
    variance = lax.optimization_barrier(jnp.mean(centred * centred, axis=-1, keepdims=True))
    return centred * lax.rsqrt(variance + NORM_EPSILON) * gain

def segment_ids(positions, bounds, limit):
    counted = lax.optimization_barrier(jnp.sum((positions[:, None] >= bounds[None, :-1]).astype(jnp.int32), axis=1))
    inside = (positions >= 0) & (positions < limit)
    return jnp.where(inside, counted, -1).astype(jnp.int32)

def conv_first(window, seg_rows, w_first):
    frame_count = (window.shape[0] - 1) // 2
    bins = window.shape[1]
    padded = jnp.pad(window.astype(jnp.float32), ((0, 0), (1, 1)))
    centre = seg_rows[1:2 * frame_count:2]
    total = jnp.zeros((frame_count, bins // 2, w_first.shape[-1]), jnp.float32)
    for step_t in range(3):
        taken = padded[step_t:step_t + 2 * frame_count - 1:2]
        same_seg = (seg_rows[step_t:step_t + 2 * frame_count - 1:2] == centre).astype(jnp.float32)
        taken = taken * same_seg[:, None]
        for step_f in range(3):
            columns = taken[:, step_f:step_f + bins - 1:2]
            total = total + columns[:, :, None] * w_first[step_t, step_f][None, None, :]
    return jnp.maximum(total, 0.0).astype(jnp.bfloat16)

def conv_second(first, seg_first, w_second):
    frame_count = (first.shape[0] - 1) // 2
    channels = first.shape[2]
    quarter = first.shape[1] // 2
    padded = jnp.pad(first, ((0, 0), (1, 1), (0, 0)))
    centre = seg_first[1:2 * frame_count:2]
    total = jnp.zeros((frame_count * quarter, w_second.shape[1]), jnp.float32)
    for step_t in range(3):
        taken = padded[step_t:step_t + 2 * frame_count - 1:2]
        same_seg = (seg_first[step_t:step_t + 2 * frame_count - 1:2] == centre).astype(jnp.bfloat16)
        taken = taken * same_seg[:, None, None]
        for step_f in range(3):
            columns = taken[:, step_f:step_f + 2 * quarter - 1:2].reshape(frame_count * quarter, channels)
            offset = (step_t * 3 + step_f) * channels
            total = total + jnp.dot(columns, w_second[offset:offset + channels], preferred_element_type=jnp.float32)
    return jnp.maximum(total, 0.0).astype(jnp.bfloat16).reshape(frame_count, quarter * channels)

def local_attention(q_block, kv_block, q_seg, k_seg):
    row_count = q_block.shape[0]
    span = kv_block.shape[0]
    reach = (span - row_count) // 2
    offsets = jnp.arange(span, dtype=jnp.int32)[None, :] - jnp.arange(row_count, dtype=jnp.int32)[:, None] - reach
    allowed = (jnp.abs(offsets) <= reach) & (k_seg[None, :] == q_seg[:, None])
    q_heads = q_block.reshape(row_count, HEADS, HEAD_DIM).astype(jnp.float32)
    k_heads = kv_block[:, :WIDTH].reshape(span, HEADS, HEAD_DIM).astype(jnp.float32)
    v_heads = kv_block[:, WIDTH:].reshape(span, HEADS, HEAD_DIM).astype(jnp.float32)
    scores = jnp.einsum('qhd,khd->hqk', q_heads, k_heads) * HEAD_DIM ** (-0.5)
    scores = jnp.where(allowed[None], scores, -1e+30)
    row_max = lax.optimization_barrier(jnp.max(scores, axis=-1, keepdims=True))
    exped = jnp.where(allowed[None], jnp.exp(scores - row_max), 0.0)
    probabilities = (exped / lax.optimization_barrier(jnp.sum(exped, axis=-1, keepdims=True))).astype(jnp.bfloat16)
    context = jnp.einsum('hqk,khd->qhd', probabilities.astype(jnp.float32), v_heads)
    return context.astype(jnp.bfloat16).reshape(row_count, WIDTH)

def depthwise(gated_ext, seg_ext, seg_mid, w_depth):
    length = seg_mid.shape[0]
    total = jnp.zeros((length, gated_ext.shape[1]), jnp.float32)
    for tap_index in range(w_depth.shape[0]):
        same_seg = (seg_ext[tap_index:tap_index + length] == seg_mid).astype(jnp.float32)
        total = total + gated_ext[tap_index:tap_index + length].astype(jnp.float32) * w_depth[tap_index][None, :] * same_seg[:, None]
    return jax.nn.silu(total).astype(jnp.bfloat16)

def group_forward(mel_group, length_row, w_first, w_second, w_proj, gain_attn, w_qkv, w_out, gain_conv, w_point_in, w_depth, w_point_out, gain_out):
    bounds = jnp.cumsum(length_row).astype(jnp.int32)
    frame_total = mel_group.shape[0]
    token_total = frame_total // 4
    padded_mel = jnp.concatenate([jnp.zeros((3, MEL_BINS), mel_group.dtype), mel_group], axis=0)

    def sub_block(block):
        start = (block * CONV_BLOCK).astype(jnp.int32)
        window = lax.dynamic_slice_in_dim(padded_mel, 4 * start, 4 * CONV_BLOCK + 3, 0)
        positions = 4 * start - 3 + jnp.arange(4 * CONV_BLOCK + 3, dtype=jnp.int32)
        seg_rows = segment_ids(positions, bounds, frame_total)
        first = conv_first(window, seg_rows, w_first)
        return conv_second(first, seg_rows[1::2][:first.shape[0]], w_second)
    sub = lax.map(sub_block, jnp.arange(token_total // CONV_BLOCK, dtype=jnp.int32))
    sub = sub.reshape(token_total, sub.shape[-1])
    hidden = jnp.dot(sub, w_proj, preferred_element_type=jnp.float32)
    token_pos = jnp.arange(token_total, dtype=jnp.int32)
    token_seg = segment_ids(4 * token_pos, bounds, frame_total)
    normed = layer_norm(hidden, gain_attn).astype(jnp.bfloat16)
    mixed = jnp.dot(normed, w_qkv, preferred_element_type=jnp.float32).astype(jnp.bfloat16)
    query = mixed[:, :WIDTH]
    keyval = jnp.pad(mixed[:, WIDTH:], ((WINDOW, WINDOW), (0, 0)))
    key_seg = jnp.pad(token_seg, (WINDOW, WINDOW), constant_values=-1)
    block_rows = min(512, TOK_DEV)

    def attend(block):
        start = (block * block_rows).astype(jnp.int32)
        q_block = lax.dynamic_slice_in_dim(query, start, block_rows, 0)
        kv_block = lax.dynamic_slice_in_dim(keyval, start, block_rows + 2 * WINDOW, 0)
        q_seg = lax.dynamic_slice_in_dim(token_seg, start, block_rows, 0)
        k_seg = lax.dynamic_slice_in_dim(key_seg, start, block_rows + 2 * WINDOW, 0)
        return local_attention(q_block, kv_block, q_seg, k_seg)
    context = lax.map(attend, jnp.arange(token_total // block_rows, dtype=jnp.int32)).reshape(token_total, WIDTH)
    attended = hidden + jnp.dot(context, w_out, preferred_element_type=jnp.float32)
    normed_conv = layer_norm(attended, gain_conv).astype(jnp.bfloat16)
    upward = jnp.dot(normed_conv, w_point_in, preferred_element_type=jnp.float32)
    gated = (upward[:, :WIDTH] * jax.nn.sigmoid(upward[:, WIDTH:])).astype(jnp.bfloat16)
    reach = KERNEL // 2
    gated_ext = jnp.pad(gated, ((reach, reach), (0, 0)))
    seg_ext = jnp.pad(token_seg, (reach, reach), constant_values=-1)
    acted = depthwise(gated_ext, seg_ext, token_seg, w_depth)
    combined = attended + jnp.dot(acted, w_point_out, preferred_element_type=jnp.float32)
    return layer_norm(combined, gain_out).astype(jnp.bfloat16)

def reference(mel_frames, lengths, w_first, w_second, w_proj, gain_attn, w_qkv, w_out, gain_conv, w_point_in, w_depth, w_point_out, gain_out):

    def one_group(paired):
        return group_forward(paired[0], paired[1], w_first, w_second, w_proj, gain_attn, w_qkv, w_out, gain_conv, w_point_in, w_depth, w_point_out, gain_out)
    return lax.map(one_group, (mel_frames, lengths))
```

```python
import jax, jax.numpy as jnp
from jax import lax
from jax.experimental import pallas as pl
from jax.experimental.pallas import tpu as pltpu
from jax.sharding import PartitionSpec as P

MESH = pl.DeviceIdType.MESH
AXES = {"z": 0, "x": 1, "y": 2}
ORDERS = (("x", "y", "z"), ("y", "z", "x"), ("z", "x", "y"))
CHUNKS = (
    (0, 0, 256, 0), (1, 0, 256, 0), (1, 256, 384, 1), (1, 640, 384, 2),
    (2, 0, 1024, 0), (2, 1024, 1024, 1), (2, 2048, 1024, 2),
    (3, 0, 1024, 0), (4, 0, 384, 0), (5, 0, 1024, 1), (4, 384, 384, 1), (4, 768, 1280, 2),
)

def gather_kernel(*refs):
    n = 6
    ins, outs = refs[:n], refs[n:2 * n]
    send_sems, recv_sems, sib_send, sib_recv, local_sems = refs[2 * n:]
    z = lax.axis_index("rec")
    tm = lax.axis_index("tm")
    x, y, c = tm // 8, (tm // 2) % 4, tm % 2
    here = {"z": z, "x": x, "y": y}

    def device(pos, core):
        return {"rec": pos["z"], "tm": pos["x"] * 8 + pos["y"] * 2 + core}

    def moved(axis, step):
        pos = dict(here)
        pos[axis] = (here[axis] + step + 4) % 4
        return pos

    def place(order, stage, pos, core, half=None):
        free = ORDERS[order][: stage - 1]
        index = []
        for axis in ("z", "x", "y"):
            if axis not in free:
                index.append(pos[axis])
            elif half is not None and axis == free[0]:
                index.append(pl.ds(2 * half, 2))
            else:
                index.append(slice(None))
        return tuple(index) + (core,)

    barrier = pltpu.get_barrier_semaphore()
    for axis in ("x", "y", "z"):
        for step in (1, 2, 3):
            pl.semaphore_signal(barrier, inc=1, device_id=device(moved(axis, step), c), device_id_type=MESH)
    pl.semaphore_signal(barrier, inc=1, device_id=device(here, 1 - c), device_id_type=MESH)

    local = []
    for a in range(n):
        copy = pltpu.make_async_copy(ins[a], outs[a].at[z, x, y, c], local_sems.at[a])
        copy.start()
        local.append(copy)
    pl.semaphore_wait(barrier, 10)

    everything = []

    def remote(chunk, src, dst, slot, target):
        copy = pltpu.make_async_remote_copy(
            src_ref=src, dst_ref=dst, send_sem=send_sems.at[chunk, slot],
            recv_sem=recv_sems.at[chunk, slot], device_id=target, device_id_type=MESH)
        copy.start()
        everything.append(copy)
        return copy

    def view(chunk, index):
        a, col, cols, order = CHUNKS[chunk]
        return outs[a].at[index + (slice(None), pl.ds(col, cols))]

    def sibling(chunk, slot, stage, pos, half=None):
        order = CHUNKS[chunk][3]
        ref = view(chunk, place(order, stage, pos, c, half))
        copy = pltpu.make_async_remote_copy(
            src_ref=ref, dst_ref=ref, send_sem=sib_send.at[chunk, slot],
            recv_sem=sib_recv.at[chunk, slot], device_id=device(here, 1 - c), device_id_type=MESH)
        copy.start()
        everything.append(copy)
        return copy

    m = len(CHUNKS)
    first, second, second_b, third, third_b, sib = {}, {}, {}, {}, {}, {}
    for k, (a, col, cols, order) in enumerate(CHUNKS):
        axis = ORDERS[order][0]
        src = ins[a].at[:, pl.ds(col, cols)]
        dst = view(k, place(order, 1, here, c))
        first[k] = [remote(k, src, dst, i, device(moved(axis, step), c)) for i, step in enumerate((1, 3, 2))]
    for copy in local:
        copy.wait()
    for stage, base, store, store_b in ((2, 3, second, second_b), (3, 7, third, third_b)):
        for k, (a, col, cols, order) in enumerate(CHUNKS):
            axis = ORDERS[order][stage - 1]
            for copy in (first[k] if stage == 2 else second_b[k]):
                copy.wait_recv()
            ref = view(k, place(order, stage, here, c))
            store[k] = [remote(k, ref, ref, base + i, device(moved(axis, step), c)) for i, step in enumerate((1, 3))]
            if stage == 3:
                sib[k] = [sibling(k, 0, 3, here)]
        for k, (a, col, cols, order) in enumerate(CHUNKS):
            axis = ORDERS[order][stage - 1]
            for copy in store[k]:
                copy.wait_recv()
            store_b[k] = []
            for i, (came, goes) in enumerate(((3, 1), (1, 3))):
                ref = view(k, place(order, stage, moved(axis, came), c, i))
                store_b[k].append(remote(k, ref, ref, base + 2 + i, device(moved(axis, goes), c)))
            if stage == 3:
                sib[k].append(sibling(k, 1, 3, moved(axis, 3)))
                sib[k].append(sibling(k, 2, 3, moved(axis, 1)))
    for k, (a, col, cols, order) in enumerate(CHUNKS):
        axis = ORDERS[order][2]
        for copy in third_b[k]:
            copy.wait_recv()
        sib[k].append(sibling(k, 3, 3, moved(axis, 2)))
    for k in range(m):
        for copy in sib[k]:
            copy.wait_recv()
    for copy in everything:
        copy.wait_send()

def gather_all(shards):
    m = len(CHUNKS)
    return pl.pallas_call(
        gather_kernel,
        out_shape=[jax.ShapeDtypeStruct((4, 4, 4, 2) + s.shape, s.dtype) for s in shards],
        in_specs=[pl.BlockSpec(memory_space=pl.ANY)] * 6,
        out_specs=[pl.BlockSpec(memory_space=pl.ANY)] * 6,
        scratch_shapes=[
            pltpu.SemaphoreType.DMA((m, 11)), pltpu.SemaphoreType.DMA((m, 11)),
            pltpu.SemaphoreType.DMA((m, 4)), pltpu.SemaphoreType.DMA((m, 4)),
            pltpu.SemaphoreType.DMA((6,)),
        ],
        compiler_params=pltpu.CompilerParams(collective_id=0, has_side_effects=True, vmem_limit_bytes=4 * 2**20),
    )(*shards)

WIDTH = 1024
HEADS = 8
KERNEL = 9
WINDOW = 128
HEAD_DIM = 128
QUARTER = 20
SPAN = 41
NORM_EPSILON = 1e-05
VMEM_LIMIT = 60 * 2**20
BF16 = jnp.bfloat16
F32 = jnp.float32


def dot(a, b):
    return jnp.dot(a, b, preferred_element_type=F32)


def segments(positions, bounds, limit):
    counted = sum((positions >= b).astype(jnp.int32) for b in bounds)
    return jnp.where((positions >= 0) & (positions < limit), counted, -1)


def read_bounds(lengths_ref):
    first = lengths_ref[0, 0]
    second = first + lengths_ref[0, 1]
    return first, second, second + lengths_ref[0, 2]


def normalised(values, gain):
    centred = values - jnp.mean(values, axis=-1, keepdims=True)
    variance = jnp.mean(centred * centred, axis=-1, keepdims=True)
    return centred * lax.rsqrt(variance + NORM_EPSILON) * gain


def norm_rows(source, gain_ref, target, step=64):
    gain = gain_ref[...]

    def body(i, carry):
        rows = pl.ds(pl.multiple_of(i * step, step), step)
        target[rows, :] = normalised(source[rows, :], gain).astype(target.dtype)
        return carry

    lax.fori_loop(0, source.shape[0] // step, body, 0)


def conv_kernel(
    lengths_ref, edge_ref, mel_ref, w_first_ref, w2_ref, wp_hbm, gain_ref, wq_hbm,
    hidden_ref, mixed_ref,
    melf, x_ref, band, w2s, even, odd, sub, wp, wq, normed, sems,
):
    tokens = mel_ref.shape[0] // 4
    channels = w_first_ref.shape[-1]
    frames_all = mel_ref.shape[0] * lax.axis_size("tm")
    copy_p = pltpu.make_async_copy(wp_hbm, wp, sems.at[0])
    copy_q = pltpu.make_async_copy(wq_hbm, wq, sems.at[1])
    copy_p.start()
    copy_q.start()
    bounds = read_bounds(lengths_ref)

    melf[0:8, :] = edge_ref[...].astype(F32)
    melf[8:, :] = mel_ref[...].astype(F32)
    bins = mel_ref.shape[1]
    base = 4 * tokens * lax.axis_index("tm")
    here = base + 4 * lax.broadcasted_iota(jnp.int32, (tokens, bins), 0)
    seg_here = segments(here, bounds, frames_all)

    def frame(d):
        return melf[pl.ds(8 + d, tokens, stride=4), :]

    def same(d):
        return (segments(here + d, bounds, frames_all) == seg_here).astype(F32)

    low2, up2 = same(-2), same(2)
    rows = (
        (frame(-3) * same(-3), frame(-2) * low2, frame(-1) * low2),
        (frame(-1) * same(-1), frame(0), frame(1) * same(1)),
        (frame(1) * up2, frame(2) * up2, frame(3) * same(3)),
    )
    bin_at = lax.broadcasted_iota(jnp.int32, (bins, 256), 0)
    place = lax.broadcasted_iota(jnp.int32, (bins, 256), 1)
    half, within = place // 128, place % 128
    for v in range(3):
        total = jnp.zeros((tokens, 256), F32)
        for a in range(3):
            column = within - SPAN * a
            chosen = (column >= 0) & (column < SPAN) & (bin_at == 40 * half - 1 + column)
            total = total + dot(rows[v][a].astype(BF16), chosen.astype(F32).astype(BF16))
        total = total.astype(BF16)
        for h in range(2):
            piece = total[:, 128 * h : 128 * (h + 1)]
            x_ref[h, v * tokens : (v + 1) * tokens, 0:128] = piece
            x_ref[h, v * tokens : (v + 1) * tokens, 128:256] = piece

    row_at = lax.broadcasted_iota(jnp.int32, (256, channels), 0)
    low_part, r = row_at // 128, row_at % 128
    at = r // SPAN
    column = r - SPAN * at
    spread = []
    for b in range(3):
        value = jnp.zeros((256, channels), F32)
        for a in range(3):
            w = w_first_ref[a, b : b + 1, :]
            top = w.astype(BF16).astype(F32)
            value = jnp.where(at == a, jnp.where(low_part == 0, top, w - top), value)
        spread.append(value)

    def make_band(f, carry):
        value = jnp.zeros((256, channels), F32)
        for b in range(3):
            value = jnp.where(column == 2 * f + b, spread[b], value)
        band[f] = value.astype(BF16)
        return carry

    lax.fori_loop(0, QUARTER, make_band, 0)

    for a in range(3):
        for b in range(3):
            start = (3 * a + b) * channels
            w2s[b, a * channels : (a + 1) * channels, :] = w2_ref[start : start + channels, :]

    odd[1] = jnp.zeros(odd.shape[1:], BF16)

    def conv_step(f2, carry):
        h = f2 // 10
        f = 2 * f2 - 20 * h
        slot = f2 % 2
        for part, target in ((0, even), (1, odd.at[slot])):
            for v in range(3):
                made = dot(x_ref[h, v * tokens : (v + 1) * tokens, :], band[f + part])
                target[:, v * channels : (v + 1) * channels] = jnp.maximum(made, 0.0).astype(BF16)
        total = dot(odd[1 - slot], w2s[0]) + dot(even[...], w2s[1]) + dot(odd[slot], w2s[2])
        columns = pl.ds(pl.multiple_of(f2 * channels, channels), channels)
        sub[:, columns] = jnp.maximum(total, 0.0).astype(BF16)
        return carry

    lax.fori_loop(0, QUARTER, conv_step, 0)
    copy_p.wait()

    def proj_step(n, carry):
        columns = pl.ds(pl.multiple_of(n * 256, 256), 256)
        hidden_ref[:, columns] = dot(sub[...], wp[:, columns])
        return carry

    lax.fori_loop(0, WIDTH // 256, proj_step, 0)
    norm_rows(hidden_ref, gain_ref, normed)
    copy_q.wait()

    def mix_step(n, carry):
        columns = pl.ds(pl.multiple_of(n * 256, 256), 256)
        mixed_ref[:, columns] = dot(normed[...], wq[:, columns]).astype(BF16)
        return carry

    lax.fori_loop(0, 3 * WIDTH // 256, mix_step, 0)


def attend_kernel(
    lengths_ref, mixed_ref, low_ref, high_ref, hidden_ref, wo_ref, gain_ref, wi_ref,
    attended_ref, gated_ref,
    keyval, bias, context, normed,
):
    tokens = mixed_ref.shape[0]
    limit = 4 * tokens * lax.axis_size("tm")
    bounds = read_bounds(lengths_ref)
    base = tokens * lax.axis_index("tm")
    keyval[0:WINDOW, :] = low_ref[...]
    keyval[WINDOW : WINDOW + tokens, :] = mixed_ref[:, WIDTH:]
    keyval[WINDOW + tokens :, :] = high_ref[...]
    reach = 3 * WINDOW
    q_at = lax.broadcasted_iota(jnp.int32, (WINDOW, 1), 0)
    k_at = lax.broadcasted_iota(jnp.int32, (1, reach), 1) - WINDOW
    near = jnp.abs(k_at - q_at) <= WINDOW

    def block_step(block, carry):
        start = pl.multiple_of(block * WINDOW, WINDOW)
        q_rows, k_rows = pl.ds(start, WINDOW), pl.ds(start, reach)
        q_seg = segments(4 * (base + start + q_at), bounds, limit)
        k_seg = segments(4 * (base + start + k_at), bounds, limit)
        bias[...] = jnp.where(near & (q_seg == k_seg), 0.0, -1e30)
        for head in range(HEADS):
            own = slice(head * HEAD_DIM, (head + 1) * HEAD_DIM)
            values = slice(WIDTH + head * HEAD_DIM, WIDTH + (head + 1) * HEAD_DIM)
            scores = lax.dot_general(
                mixed_ref[q_rows, own], keyval[k_rows, own], (((1,), (1,)), ((), ())),
                preferred_element_type=F32,
            ) * HEAD_DIM ** (-0.5) + bias[...]
            exped = jnp.exp(scores - jnp.max(scores, axis=-1, keepdims=True))
            share = 1.0 / jnp.sum(exped, axis=-1, keepdims=True)
            context[q_rows, own] = dot((exped * share).astype(BF16), keyval[k_rows, values]).astype(BF16)
        return carry

    lax.fori_loop(0, tokens // WINDOW, block_step, 0)

    def out_step(n, carry):
        columns = pl.ds(pl.multiple_of(n * 256, 256), 256)
        attended_ref[:, columns] = hidden_ref[:, columns] + dot(context[...], wo_ref[:, columns])
        return carry

    lax.fori_loop(0, WIDTH // 256, out_step, 0)
    norm_rows(attended_ref, gain_ref, normed)

    def gate_step(n, carry):
        start = pl.multiple_of(n * 256, 256)
        value = dot(normed[...], wi_ref[:, pl.ds(start, 256)])
        gate = dot(normed[...], wi_ref[:, pl.ds(WIDTH + start, 256)])
        gated_ref[:, pl.ds(start, 256)] = (value * jax.nn.sigmoid(gate)).astype(BF16)
        return carry

    lax.fori_loop(0, WIDTH // 256, gate_step, 0)


def depth_kernel(
    lengths_ref, gated_ref, low_ref, high_ref, w_depth_ref, attended_ref, wu_ref, gain_ref,
    out_ref,
    extended, acted, combined,
):
    tokens = gated_ref.shape[0]
    limit = 4 * tokens * lax.axis_size("tm")
    bounds = read_bounds(lengths_ref)
    base = tokens * lax.axis_index("tm")
    extended[0:8, :] = low_ref[...].astype(F32)
    extended[8 : 8 + tokens, :] = gated_ref[...].astype(F32)
    extended[8 + tokens :, :] = high_ref[...].astype(F32)
    block = 64
    reach = KERNEL // 2

    def depth_step(i, carry):
        start = pl.multiple_of(i * block, block)
        position = base + start + lax.broadcasted_iota(jnp.int32, (block, 1), 0)
        own = segments(4 * position, bounds, limit)
        same = [
            (segments(4 * (position + k - reach), bounds, limit) == own).astype(F32)
            for k in range(KERNEL)
        ]
        for n in range(WIDTH // 256):
            columns = slice(n * 256, (n + 1) * 256)
            window = extended[pl.ds(start, block + 16), columns]
            total = jnp.zeros((block, 256), F32)
            for k in range(KERNEL):
                taken = window[4 + k : 4 + k + block]
                total = total + taken * w_depth_ref[k : k + 1, columns] * same[k]
            acted[pl.ds(start, block), columns] = (total * jax.nn.sigmoid(total)).astype(BF16)
        return carry

    lax.fori_loop(0, tokens // block, depth_step, 0)

    def out_step(n, carry):
        columns = pl.ds(pl.multiple_of(n * 256, 256), 256)
        combined[:, columns] = attended_ref[:, columns] + dot(acted[...], wu_ref[:, columns])
        return carry

    lax.fori_loop(0, WIDTH // 256, out_step, 0)
    norm_rows(combined, gain_ref, out_ref)


def along(block, step):
    devices = range(lax.axis_size("tm"))
    return lax.ppermute(block, "tm", [(i, i + step) for i in devices if i + step in devices])


def call(kernel, outs, scratch, specs, *args):
    vmem = pl.BlockSpec(memory_space=pltpu.VMEM)
    return pl.pallas_call(
        kernel,
        out_shape=outs,
        in_specs=[vmem if s is None else pl.BlockSpec(memory_space=s) for s in specs],
        out_specs=[vmem] * len(outs),
        scratch_shapes=scratch,
        compiler_params=pltpu.CompilerParams(vmem_limit_bytes=VMEM_LIMIT),
    )(*args)


def on_device(
    mel_frames, lengths, w_first, w_second, w_proj, gain_attn, w_qkv, w_out, gain_conv,
    w_point_in, w_depth, w_point_out, gain_out,
):
    mel = mel_frames[0]
    tokens = mel.shape[0] // 4
    bins = mel.shape[1]
    channels = w_first.shape[-1]
    parts = gather_all((w_second, w_proj, w_qkv, w_out, w_point_in, w_point_out))
    w2, wp, wq, wo, wi, wu = [
        part.reshape(128 * part.shape[4], part.shape[5]) for part in parts
    ]
    gain_attn, gain_conv, gain_out = (g[None] for g in (gain_attn, gain_conv, gain_out))
    edge = along(mel[-8:], 1)
    hidden, mixed = call(
        conv_kernel,
        [jax.ShapeDtypeStruct((tokens, WIDTH), F32), jax.ShapeDtypeStruct((tokens, 3 * WIDTH), BF16)],
        [
            pltpu.VMEM((4 * tokens + 8, bins), F32),
            pltpu.VMEM((2, 3 * tokens, 256), BF16),
            pltpu.VMEM((QUARTER, 256, channels), BF16),
            pltpu.VMEM((3, 3 * channels, channels), BF16),
            pltpu.VMEM((tokens, 3 * channels), BF16),
            pltpu.VMEM((2, tokens, 3 * channels), BF16),
            pltpu.VMEM((tokens, QUARTER * channels), BF16),
            pltpu.VMEM(wp.shape, BF16),
            pltpu.VMEM(wq.shape, BF16),
            pltpu.VMEM((tokens, WIDTH), BF16),
            pltpu.SemaphoreType.DMA((2,)),
        ],
        [pltpu.SMEM, None, None, None, None, pl.ANY, None, pl.ANY],
        lengths, edge, mel, w_first, w2, wp, gain_attn, wq,
    )
    low = along(mixed[tokens - WINDOW :, WIDTH:], 1)
    high = along(mixed[:WINDOW, WIDTH:], -1)
    attended, gated = call(
        attend_kernel,
        [jax.ShapeDtypeStruct((tokens, WIDTH), F32), jax.ShapeDtypeStruct((tokens, WIDTH), BF16)],
        [
            pltpu.VMEM((tokens + 2 * WINDOW, 2 * WIDTH), BF16),
            pltpu.VMEM((WINDOW, 3 * WINDOW), F32),
            pltpu.VMEM((tokens, WIDTH), BF16),
            pltpu.VMEM((tokens, WIDTH), BF16),
        ],
        [pltpu.SMEM] + [None] * 7,
        lengths, mixed, low, high, hidden, wo, gain_conv, wi,
    )
    low = along(gated[tokens - 8 :], 1)
    high = along(gated[:8], -1)
    (encoded,) = call(
        depth_kernel,
        [jax.ShapeDtypeStruct((tokens, WIDTH), BF16)],
        [
            pltpu.VMEM((tokens + 16, WIDTH), F32),
            pltpu.VMEM((tokens, WIDTH), BF16),
            pltpu.VMEM((tokens, WIDTH), F32),
        ],
        [pltpu.SMEM] + [None] * 7,
        lengths, gated, low, high, w_depth, attended, wu, gain_out,
    )
    return encoded[None]


def solution(mesh):
    weight = P(("rec", "tm"), None)
    placed = (
        P("rec", "tm", None), P("rec", None), P(), weight, weight, P(), weight, weight, P(),
        weight, P(), weight, P(),
    )
    return jax.shard_map(
        on_device, mesh=mesh, in_specs=placed, out_specs=P("rec", "tm", None), check_vma=False
    )
```

```python
import jax
import jax.numpy as jnp
from jax import lax
from jax.experimental import pallas as pl
from jax.experimental.pallas import tpu as pltpu
from jax.sharding import PartitionSpec as P

WIDTH = 1024
HEADS = 8
KERNEL = 9
WINDOW = 128
HEAD_DIM = 128
QUARTER = 20
SPAN = 41
NORM_EPSILON = 1e-05
VMEM_LIMIT = 62 * 2**20
BF16 = jnp.bfloat16
F32 = jnp.float32
MESH = pl.DeviceIdType.MESH

ORDERS = (("x", "y", "z"), ("y", "z", "x"), ("z", "x", "y"))
CHUNKS = (
    (0, 0, 256, 0),
    (1, 0, 256, 0), (1, 256, 384, 1), (1, 640, 384, 2),
    (2, 0, 1024, 0), (2, 1024, 1024, 1), (2, 2048, 1024, 2),
    (3, 0, 1024, 0), (4, 0, 384, 0), (5, 0, 1024, 1), (4, 384, 384, 1), (4, 768, 1280, 2),
)
PHASES = ((0,), (1, 2, 3), (4, 5, 6), (7, 8, 9, 10, 11))
LOOP_STEPS = {
    0: ((1, 3),), 1: ((2, 2),), 2: ((1, 4),), 3: ((3, 1),), 4: ((2, 3),), 6: ((2, 4), (3, 2)),
    7: ((1, 5),), 9: ((3, 3),), 11: ((1, 6), (3, 4)), 12: ((2, 5),), 14: ((1, 7),), 16: ((2, 6),),
    17: ((3, 5),), 19: ((2, 7),),
}
SLOTS = 15


def dot(a, b):
    return jnp.dot(a, b, preferred_element_type=F32)


def segments(positions, bounds, limit):
    counted = sum((positions >= b).astype(jnp.int32) for b in bounds)
    return jnp.where((positions >= 0) & (positions < limit), counted, -1)


def normalised(values, gain):
    centred = values - jnp.mean(values, axis=-1, keepdims=True)
    variance = jnp.mean(centred * centred, axis=-1, keepdims=True)
    return centred * lax.rsqrt(variance + NORM_EPSILON) * gain


def norm_rows(source, gain_ref, target, step=64):
    gain = gain_ref[...]

    def body(i, carry):
        rows = pl.ds(pl.multiple_of(i * step, step), step)
        target[rows, :] = normalised(source[rows, :], gain).astype(target.dtype)
        return carry

    lax.fori_loop(0, source.shape[0] // step, body, 0)


def over_columns(count, body, first=0):
    def step(n, carry):
        body(pl.multiple_of(n * 256, 256))
        return carry

    lax.fori_loop(first, count, step, 0)


class Gather:
    def __init__(self, shards, wholes, send_sems, recv_sems):
        self.shards, self.wholes = shards, wholes
        self.send_sems, self.recv_sems = send_sems, recv_sems
        tm = lax.axis_index("tm")
        self.here = {"z": lax.axis_index("rec"), "x": tm // 8, "y": (tm // 2) % 4}
        self.core = tm % 2
        self.near = {
            (axis, step): {**self.here, axis: (self.here[axis] + step) % 4}
            for axis in ("x", "y", "z")
            for step in (1, 2, 3)
        }

    def device(self, position, core):
        return {"rec": position["z"], "tm": position["x"] * 8 + position["y"] * 2 + core}

    def peers(self):
        chips = [self.device(position, self.core) for position in self.near.values()]
        return chips + [self.device(self.here, 1 - self.core)]

    def view(self, chunk, stage, position, half=None):
        array, column, columns, order = CHUNKS[chunk]
        free = ORDERS[order][: stage - 1]
        index = []
        for axis in ("z", "x", "y"):
            if axis not in free:
                index.append(position[axis])
            elif half is not None and axis == free[0]:
                index.append(pl.ds(2 * half, 2))
            else:
                index.append(slice(None))
        return self.wholes[array].at[tuple(index) + (self.core, slice(None), pl.ds(column, columns))]

    def copy(self, chunk, slot):
        array, column, columns, order = CHUNKS[chunk]
        axes = ORDERS[order]
        target = None
        if slot < 3:
            target = self.near[axes[0], (1, 3, 2)[slot]]
            source = self.shards[array].at[:, pl.ds(column, columns)]
            place = self.view(chunk, 1, self.here)
        elif slot < 11:
            stage = 2 if slot < 7 else 3
            axis = axes[stage - 1]
            at = (slot - 3) % 4
            target = self.near[axis, (1, 3, 1, 3)[at]]
            if at < 2:
                source = self.view(chunk, stage, self.here)
            else:
                source = self.view(chunk, stage, self.near[axis, (3, 1)[at - 2]], at - 2)
            place = source
        else:
            axis = axes[2]
            at = slot - 11
            source = self.view(chunk, 3, self.here if at == 0 else self.near[axis, (3, 1, 2)[at - 1]])
            place = source
        where = self.device(self.here, 1 - self.core) if target is None else self.device(target, self.core)
        return pltpu.make_async_remote_copy(
            src_ref=source, dst_ref=place, send_sem=self.send_sems.at[chunk, slot],
            recv_sem=self.recv_sems.at[chunk, slot], device_id=where, device_id_type=MESH,
        )

    def step(self, phase, number):
        awaited = ((), (0, 1, 2), (3, 4), (5, 6), (7, 8), (9, 10), (11, 12, 13, 14))[number - 1]
        started = ((0, 1, 2), (3, 4), (5, 6), (7, 8, 11), (9, 10, 12, 13), (14,), ())[number - 1]
        for chunk in PHASES[phase]:
            for slot in awaited:
                self.copy(chunk, slot).wait_recv()
            for slot in started:
                self.copy(chunk, slot).start()

    def finish(self):
        for chunk in range(len(CHUNKS)):
            for slot in range(SLOTS):
                self.copy(chunk, slot).wait_send()


def block_kernel(
    lengths_ref, mel_ref, w_first_ref, gain_attn_ref, gain_conv_ref, w_depth_ref, gain_out_ref,
    ws_shard, wp_shard, wq_shard, wo_shard, wi_shard, wu_shard,
    out_ref,
    edge, melf, x_ref, band, ws, wp, wq, wo, wi, wu, w2, w2s, even, odd, sub,
    hidden, normed, query, keyval, bias, context, extended,
    send_sems, recv_sems, own_sems, halo_send, halo_recv,
):
    tokens = mel_ref.shape[0] // 4
    channels = w_first_ref.shape[-1]
    bins = mel_ref.shape[1]
    tm = lax.axis_index("tm")
    count = lax.axis_size("tm")
    rec = lax.axis_index("rec")
    frames_all = mel_ref.shape[0] * count
    shards = (ws_shard, wp_shard, wq_shard, wo_shard, wi_shard, wu_shard)
    wholes = (ws, wp, wq, wo, wi, wu)
    gather = Gather(shards, wholes, send_sems, recv_sems)
    after = {"rec": rec, "tm": (tm + 1) % count}
    before = {"rec": rec, "tm": (tm + count - 1) % count}

    barrier = pltpu.get_barrier_semaphore()
    greeted = gather.peers() + [after, before]
    for device in greeted:
        pl.semaphore_signal(barrier, inc=1, device_id=device, device_id_type=MESH)

    def own_copy(array):
        here = gather.here
        place = wholes[array].at[here["z"], here["x"], here["y"], gather.core]
        return pltpu.make_async_copy(shards[array], place, own_sems.at[array])

    for array in range(6):
        own_copy(array).start()
    pl.semaphore_wait(barrier, len(greeted))

    def pass_on(source, place, device, number):
        return pltpu.make_async_remote_copy(
            src_ref=source, dst_ref=place, send_sem=halo_send.at[number],
            recv_sem=halo_recv.at[number], device_id=device, device_id_type=MESH,
        )

    def weight(array, start):
        whole = wholes[array]
        value = whole[:, :, :, :, :, pl.ds(start, 256)]
        return value.reshape(128 * whole.shape[4], 256)

    gather.step(0, 1)
    edge_copy = pass_on(mel_ref.at[pl.ds(4 * tokens - 8, 8), :], edge, after, 0)
    edge_copy.start()
    gather.step(1, 1)
    gather.step(2, 1)
    for array in range(6):
        own_copy(array).wait()

    first = lengths_ref[0, 0]
    second = first + lengths_ref[0, 1]
    bounds = (first, second, second + lengths_ref[0, 2])

    row_at = lax.broadcasted_iota(jnp.int32, (256, channels), 0)
    low_part, r = row_at // 128, row_at % 128
    at = r // SPAN
    column = r - SPAN * at
    spread = []
    for b in range(3):
        value = jnp.zeros((256, channels), F32)
        for a in range(3):
            w = w_first_ref[a, b : b + 1, :]
            top = w.astype(BF16).astype(F32)
            value = jnp.where(at == a, jnp.where(low_part == 0, top, w - top), value)
        spread.append(value)

    gather.step(0, 2)

    def make_band(f, carry):
        value = jnp.zeros((256, channels), F32)
        for b in range(3):
            value = jnp.where(column == 2 * f + b, spread[b], value)
        band[f] = value.astype(BF16)
        return carry

    lax.fori_loop(0, QUARTER // 2, make_band, 0)
    gather.step(0, 3)
    lax.fori_loop(QUARTER // 2, QUARTER, make_band, 0)
    gather.step(0, 4)
    edge_copy.wait_recv()

    melf[0:8, :] = edge[...].astype(F32)
    melf[8:, :] = mel_ref[...].astype(F32)
    frame_at = 4 * tokens * tm + 4 * lax.broadcasted_iota(jnp.int32, (tokens, bins), 0)
    seg_here = segments(frame_at, bounds, frames_all)

    def frame(d):
        return melf[pl.ds(8 + d, tokens, stride=4), :]

    def same(d):
        return (segments(frame_at + d, bounds, frames_all) == seg_here).astype(F32)

    low2, up2 = same(-2), same(2)
    rows = (
        (frame(-3) * same(-3), frame(-2) * low2, frame(-1) * low2),
        (frame(-1) * same(-1), frame(0), frame(1) * same(1)),
        (frame(1) * up2, frame(2) * up2, frame(3) * same(3)),
    )
    bin_at = lax.broadcasted_iota(jnp.int32, (bins, 256), 0)
    place = lax.broadcasted_iota(jnp.int32, (bins, 256), 1)
    half, within = place // 128, place % 128
    for v in range(3):
        total = jnp.zeros((tokens, 256), F32)
        for a in range(3):
            taken = within - SPAN * a
            chosen = (taken >= 0) & (taken < SPAN) & (bin_at == 40 * half - 1 + taken)
            total = total + dot(rows[v][a].astype(BF16), chosen.astype(F32).astype(BF16))
        total = total.astype(BF16)
        for h in range(2):
            piece = total[:, 128 * h : 128 * (h + 1)]
            x_ref[h, v * tokens : (v + 1) * tokens, 0:128] = piece
            x_ref[h, v * tokens : (v + 1) * tokens, 128:256] = piece
        if v == 0:
            gather.step(0, 5)
        if v == 1:
            gather.step(0, 6)

    gather.step(1, 2)
    gather.step(0, 7)
    depth = ws.shape[4]

    def unpack(i, carry):
        group = w2.at[pl.ds(pl.multiple_of(8 * depth * i, 16), 8 * depth), :]
        for s in range(8):
            group[s * depth : (s + 1) * depth, :] = ws[i // 4, i % 4, s // 2, s % 2]
        return carry

    lax.fori_loop(0, 16, unpack, 0)
    for a in range(3):
        for b in range(3):
            start = (3 * a + b) * channels
            w2s[b, a * channels : (a + 1) * channels, :] = w2[start : start + channels, :]

    odd[1] = jnp.zeros(odd.shape[1:], BF16)

    def conv_step(f2, carry):
        for number, pairs in LOOP_STEPS.items():

            @pl.when(f2 == number)
            def _():
                for phase, step in pairs:
                    gather.step(phase, step)

        h = f2 // 10
        f = 2 * f2 - 20 * h
        slot = f2 % 2
        for part, target in ((0, even), (1, odd.at[slot])):
            for v in range(3):
                made = dot(x_ref[h, v * tokens : (v + 1) * tokens, :], band[f + part])
                target[:, v * channels : (v + 1) * channels] = jnp.maximum(made, 0.0).astype(BF16)
        total = dot(odd[1 - slot], w2s[0]) + dot(even[...], w2s[1]) + dot(odd[slot], w2s[2])
        columns = pl.ds(pl.multiple_of(f2 * channels, channels), channels)
        sub[:, columns] = jnp.maximum(total, 0.0).astype(BF16)
        return carry

    lax.fori_loop(0, QUARTER, conv_step, 0)

    def project(start):
        columns = pl.ds(start, 256)
        hidden[:, columns] = dot(sub[...], weight(1, start))

    over_columns(2, project)
    gather.step(3, 6)
    over_columns(4, project, 2)
    norm_rows(hidden, gain_attn_ref, normed)

    def mix_keyval(start):
        keyval[WINDOW : WINDOW + tokens, pl.ds(start, 256)] = dot(
            normed[...], weight(2, WIDTH + start)
        ).astype(BF16)

    over_columns(2 * WIDTH // 256, mix_keyval)
    halos = (
        pass_on(keyval.at[pl.ds(tokens, WINDOW), :], keyval.at[pl.ds(0, WINDOW), :], after, 1),
        pass_on(
            keyval.at[pl.ds(WINDOW, WINDOW), :], keyval.at[pl.ds(WINDOW + tokens, WINDOW), :], before, 2
        ),
    )
    for copy in halos:
        copy.start()
    gather.step(3, 7)

    def mix_query(start):
        query[:, pl.ds(start, 256)] = dot(normed[...], weight(2, start)).astype(BF16)

    over_columns(WIDTH // 256, mix_query)

    base = tokens * tm
    reach = 3 * WINDOW
    q_at = lax.broadcasted_iota(jnp.int32, (WINDOW, 1), 0)
    k_at = lax.broadcasted_iota(jnp.int32, (1, reach), 1) - WINDOW
    near = jnp.abs(k_at - q_at) <= WINDOW
    blocks = tokens // WINDOW

    def attend(i, carry):
        block = (i + 1) % blocks

        @pl.when(i == blocks - 2)
        def _():
            for copy in halos:
                copy.wait_recv()

        start = pl.multiple_of(block * WINDOW, WINDOW)
        q_rows, k_rows = pl.ds(start, WINDOW), pl.ds(start, reach)
        q_seg = segments(4 * (base + start + q_at), bounds, frames_all)
        k_seg = segments(4 * (base + start + k_at), bounds, frames_all)
        bias[...] = jnp.where(near & (q_seg == k_seg), 0.0, -1e30)
        for head in range(HEADS):
            own = slice(head * HEAD_DIM, (head + 1) * HEAD_DIM)
            values = slice(WIDTH + head * HEAD_DIM, WIDTH + (head + 1) * HEAD_DIM)
            scores = lax.dot_general(
                query[q_rows, own], keyval[k_rows, own], (((1,), (1,)), ((), ())),
                preferred_element_type=F32,
            ) * HEAD_DIM ** (-0.5) + bias[...]
            exped = jnp.exp(scores - jnp.max(scores, axis=-1, keepdims=True))
            share = 1.0 / jnp.sum(exped, axis=-1, keepdims=True)
            context[q_rows, own] = dot((exped * share).astype(BF16), keyval[k_rows, values]).astype(BF16)
        return carry

    lax.fori_loop(0, blocks, attend, 0)

    def attend_out(start):
        columns = pl.ds(start, 256)
        hidden[:, columns] = hidden[:, columns] + dot(context[...], weight(3, start))

    over_columns(WIDTH // 256, attend_out)
    norm_rows(hidden, gain_conv_ref, normed)

    def gate(start):
        value = dot(normed[...], weight(4, start))
        opening = dot(normed[...], weight(4, WIDTH + start))
        gated = (value * jax.nn.sigmoid(opening)).astype(BF16)
        extended[8 : 8 + tokens, pl.ds(start, 256)] = gated.astype(F32)

    over_columns(WIDTH // 256, gate)
    edges = (
        pass_on(extended.at[pl.ds(tokens, 8), :], extended.at[pl.ds(0, 8), :], after, 3),
        pass_on(extended.at[pl.ds(8, 8), :], extended.at[pl.ds(8 + tokens, 8), :], before, 4),
    )
    for copy in edges:
        copy.start()
    rows_at_once = 64
    groups = tokens // rows_at_once
    reach = KERNEL // 2

    def depth_step(i, carry):
        group = (i + 1) % groups

        @pl.when(i == groups - 2)
        def _():
            for copy in edges:
                copy.wait_recv()

        start = pl.multiple_of(group * rows_at_once, rows_at_once)
        position = base + start + lax.broadcasted_iota(jnp.int32, (rows_at_once, 1), 0)
        own = segments(4 * position, bounds, frames_all)
        kept = [
            (segments(4 * (position + k - reach), bounds, frames_all) == own).astype(F32)
            for k in range(KERNEL)
        ]
        for n in range(WIDTH // 256):
            columns = slice(n * 256, (n + 1) * 256)
            window = extended[pl.ds(start, rows_at_once + 16), columns]
            total = jnp.zeros((rows_at_once, 256), F32)
            for k in range(KERNEL):
                taken = window[4 + k : 4 + k + rows_at_once]
                total = total + taken * w_depth_ref[k : k + 1, columns] * kept[k]
            context[pl.ds(start, rows_at_once), columns] = (total * jax.nn.sigmoid(total)).astype(BF16)
        return carry

    lax.fori_loop(0, groups, depth_step, 0)

    def point_out(start):
        columns = pl.ds(start, 256)
        hidden[:, columns] = hidden[:, columns] + dot(context[...], weight(5, start))

    over_columns(WIDTH // 256, point_out)
    norm_rows(hidden, gain_out_ref, out_ref)
    gather.finish()
    for copy in (edge_copy,) + halos + edges:
        copy.wait_send()


def on_device(
    mel_frames, lengths, w_first, w_second, w_proj, gain_attn, w_qkv, w_out, gain_conv,
    w_point_in, w_depth, w_point_out, gain_out,
):
    mel = mel_frames[0]
    tokens = mel.shape[0] // 4
    bins = mel.shape[1]
    channels = w_first.shape[-1]
    shards = (w_second, w_proj, w_qkv, w_out, w_point_in, w_point_out)
    vmem = pl.BlockSpec(memory_space=pltpu.VMEM)
    hbm = pl.BlockSpec(memory_space=pl.ANY)
    (encoded,) = pl.pallas_call(
        block_kernel,
        out_shape=[jax.ShapeDtypeStruct((tokens, WIDTH), BF16)],
        in_specs=[pl.BlockSpec(memory_space=pltpu.SMEM)] + [vmem] * 6 + [hbm] * 6,
        out_specs=[vmem],
        scratch_shapes=[
            pltpu.VMEM((8, bins), BF16),
            pltpu.VMEM((4 * tokens + 8, bins), F32),
            pltpu.VMEM((2, 3 * tokens, 256), BF16),
            pltpu.VMEM((QUARTER, 256, channels), BF16),
            *[pltpu.VMEM((4, 4, 4, 2) + s.shape, BF16) for s in shards],
            pltpu.VMEM((9 * channels, channels), BF16),
            pltpu.VMEM((3, 3 * channels, channels), BF16),
            pltpu.VMEM((tokens, 3 * channels), BF16),
            pltpu.VMEM((2, tokens, 3 * channels), BF16),
            pltpu.VMEM((tokens, QUARTER * channels), BF16),
            pltpu.VMEM((tokens, WIDTH), F32),
            pltpu.VMEM((tokens, WIDTH), BF16),
            pltpu.VMEM((tokens, WIDTH), BF16),
            pltpu.VMEM((tokens + 2 * WINDOW, 2 * WIDTH), BF16),
            pltpu.VMEM((WINDOW, 3 * WINDOW), F32),
            pltpu.VMEM((tokens, WIDTH), BF16),
            pltpu.VMEM((tokens + 16, WIDTH), F32),
            pltpu.SemaphoreType.DMA((len(CHUNKS), SLOTS)),
            pltpu.SemaphoreType.DMA((len(CHUNKS), SLOTS)),
            pltpu.SemaphoreType.DMA((6,)),
            pltpu.SemaphoreType.DMA((5,)),
            pltpu.SemaphoreType.DMA((5,)),
        ],
        compiler_params=pltpu.CompilerParams(
            collective_id=0, has_side_effects=True, vmem_limit_bytes=VMEM_LIMIT
        ),
    )(
        lengths, mel, w_first, gain_attn[None], gain_conv[None], w_depth, gain_out[None], *shards
    )
    return encoded[None]


def solution(mesh):
    weight = P(("rec", "tm"), None)
    placed = (
        P("rec", "tm", None), P("rec", None), P(), weight, weight, P(), weight, weight, P(),
        weight, P(), weight, P(),
    )
    return jax.shard_map(
        on_device, mesh=mesh, in_specs=placed, out_specs=P("rec", "tm", None), check_vma=False
    )
```

```python
import jax
import jax.numpy as jnp
from jax import lax
from jax.experimental import pallas as pl
from jax.experimental.pallas import tpu as pltpu
from jax.sharding import PartitionSpec as P

WIDTH = 1024
HEADS = 8
KERNEL = 9
WINDOW = 128
HEAD_DIM = 128
QUARTER = 20
SPAN = 41
NORM_EPSILON = 1e-05
VMEM_LIMIT = 62 * 2**20
BF16 = jnp.bfloat16
F32 = jnp.float32
MESH = pl.DeviceIdType.MESH

ORDERS = (("x", "y", "z"), ("y", "z", "x"), ("z", "x", "y"))
CHUNKS = (
    (0, 0, 128, 0), (0, 128, 128, 1),
    (1, 0, 256, 0), (1, 256, 384, 1), (1, 640, 384, 2),
    (2, 0, 1024, 0), (2, 1024, 1024, 1), (2, 2048, 1024, 2),
    (3, 0, 1024, 0), (4, 0, 384, 0), (5, 0, 1024, 1), (4, 384, 384, 1), (4, 768, 1280, 2),
)
PHASES = ((0, 1), (2, 3, 4), (5, 6, 7), (8, 9, 10, 11, 12))
DIRECT = (
    ((), (0, 1, 2)), ((0, 1, 2), (3, 4, 5)), ((3, 4, 5), (6, 7, 8, 9)), ((6, 7, 8), (10, 11, 12)),
    ((9, 10, 11, 12), ()),
)
FORWARDED = (
    ((), (0, 1, 2)), ((0, 1, 2), (3, 4)), ((3, 4), (5, 6)), ((5, 6), (7, 8, 11)),
    ((7, 8), (9, 10, 12, 13)), ((9, 10), (14,)), ((11, 12, 13, 14), ()),
)
FIRST_STEPS = {
    0: ((0, 2),), 1: ((2, 1),), 2: ((1, 2),), 5: ((3, 1),), 8: ((0, 3),), 9: ((2, 2),), 12: ((1, 3),),
    14: ((3, 2),), 16: ((2, 3),), 18: ((0, 4),), 19: ((1, 4),),
}
SECOND_STEPS = {
    1: ((3, 3),), 3: ((2, 4),), 8: ((3, 4),), 11: ((1, 5),), 18: ((1, 6),), 19: ((2, 5),),
}
SLOTS = 15


def dot(a, b):
    return jnp.dot(a, b, preferred_element_type=F32)


def segments(positions, bounds, limit):
    counted = sum((positions >= b).astype(jnp.int32) for b in bounds)
    return jnp.where((positions >= 0) & (positions < limit), counted, -1)


def normalised(values, gain):
    centred = values - jnp.mean(values, axis=-1, keepdims=True)
    variance = jnp.mean(centred * centred, axis=-1, keepdims=True)
    return centred * lax.rsqrt(variance + NORM_EPSILON) * gain


def norm_rows(source, gain_ref, target, step=64):
    gain = gain_ref[...]

    def body(i, carry):
        rows = pl.ds(pl.multiple_of(i * step, step), step)
        target[rows, :] = normalised(source[rows, :], gain).astype(target.dtype)
        return carry

    lax.fori_loop(0, source.shape[0] // step, body, 0)


def over_columns(count, body, first=0):
    def step(n, carry):
        body(pl.multiple_of(n * 256, 256))
        return carry

    lax.fori_loop(first, count, step, 0)


class Gather:
    def __init__(self, shards, wholes, send_sems, recv_sems):
        self.shards, self.wholes = shards, wholes
        self.send_sems, self.recv_sems = send_sems, recv_sems
        tm = lax.axis_index("tm")
        self.here = {"z": lax.axis_index("rec"), "x": tm // 8, "y": (tm // 2) % 4}
        self.core = tm % 2
        self.near = {
            (axis, step): {**self.here, axis: (self.here[axis] + step) % 4}
            for axis in ("x", "y", "z")
            for step in (1, 2, 3)
        }

    def device(self, position, core):
        return {"rec": position["z"], "tm": position["x"] * 8 + position["y"] * 2 + core}

    def peers(self):
        chips = [self.device(position, self.core) for position in self.near.values()]
        return chips + [self.device(self.here, 1 - self.core)]

    def view(self, chunk, stage, position, half=None):
        array, column, columns, order = CHUNKS[chunk]
        free = ORDERS[order][: stage - 1]
        index = []
        for axis in ("z", "x", "y"):
            if axis not in free:
                index.append(position[axis])
            elif half is not None and axis == free[0]:
                index.append(pl.ds(2 * half, 2))
            else:
                index.append(slice(None))
        return self.wholes[array].at[tuple(index) + (self.core, slice(None), pl.ds(column, columns))]

    def copy(self, chunk, slot):
        array, column, columns, order = CHUNKS[chunk]
        axes = ORDERS[order]
        target = None
        direct = chunk in PHASES[0]
        siblings = 9 if direct else 11
        if slot < 3:
            target = self.near[axes[0], (1, 3, 2)[slot]]
            source = self.shards[array].at[:, pl.ds(column, columns)]
            place = self.view(chunk, 1, self.here)
        elif slot < siblings and direct:
            stage = 2 if slot < 6 else 3
            target = self.near[axes[stage - 1], (1, 3, 2)[slot % 3]]
            source = self.view(chunk, stage, self.here)
            place = source
        elif slot < siblings:
            stage = 2 if slot < 7 else 3
            axis = axes[stage - 1]
            at = (slot - 3) % 4
            target = self.near[axis, (1, 3, 1, 3)[at]]
            if at < 2:
                source = self.view(chunk, stage, self.here)
            else:
                source = self.view(chunk, stage, self.near[axis, (3, 1)[at - 2]], at - 2)
            place = source
        else:
            axis = axes[2]
            at = slot - siblings
            source = self.view(chunk, 3, self.here if at == 0 else self.near[axis, (3, 1, 2)[at - 1]])
            place = source
        where = self.device(self.here, 1 - self.core) if target is None else self.device(target, self.core)
        return pltpu.make_async_remote_copy(
            src_ref=source, dst_ref=place, send_sem=self.send_sems.at[chunk, slot],
            recv_sem=self.recv_sems.at[chunk, slot], device_id=where, device_id_type=MESH,
        )

    def step(self, phase, number):
        awaited, started = (DIRECT if phase == 0 else FORWARDED)[number - 1]
        for chunk in PHASES[phase]:
            for slot in awaited:
                self.copy(chunk, slot).wait_recv()
            for slot in started:
                self.copy(chunk, slot).start()

    def finish(self):
        for chunk in range(len(CHUNKS)):
            for slot in range(13 if chunk in PHASES[0] else SLOTS):
                self.copy(chunk, slot).wait_send()


def block_kernel(
    lengths_ref, mel_ref, w_first_ref, gain_attn_ref, gain_conv_ref, w_depth_ref, gain_out_ref,
    ws_shard, wp_shard, wq_shard, wo_shard, wi_shard, wu_shard,
    out_ref, spilled,
    edge, melf, x_ref, band, ws, wp, wq, wo, wi, wu, w2, w2s, pairs, sub,
    hidden, normed, query, keyval, bias, context, extended,
    send_sems, recv_sems, own_sems, halo_send, halo_recv, spill_sems, fetch_sems,
):
    tokens = mel_ref.shape[0] // 4
    channels = w_first_ref.shape[-1]
    bins = mel_ref.shape[1]
    tm = lax.axis_index("tm")
    count = lax.axis_size("tm")
    rec = lax.axis_index("rec")
    frames_all = mel_ref.shape[0] * count
    shards = (ws_shard, wp_shard, wq_shard, wo_shard, wi_shard, wu_shard)
    wholes = (ws, wp, wq, wo, wi, wu)
    gather = Gather(shards, wholes, send_sems, recv_sems)
    after = {"rec": rec, "tm": (tm + 1) % count}
    before = {"rec": rec, "tm": (tm + count - 1) % count}

    barrier = pltpu.get_barrier_semaphore()
    greeted = gather.peers() + [after, before]
    for device in greeted:
        pl.semaphore_signal(barrier, inc=1, device_id=device, device_id_type=MESH)

    def own_copy(array):
        here = gather.here
        place = wholes[array].at[here["z"], here["x"], here["y"], gather.core]
        return pltpu.make_async_copy(shards[array], place, own_sems.at[array])

    for array in range(6):
        own_copy(array).start()

    def pass_on(source, place, device, number):
        return pltpu.make_async_remote_copy(
            src_ref=source, dst_ref=place, send_sem=halo_send.at[number],
            recv_sem=halo_recv.at[number], device_id=device, device_id_type=MESH,
        )

    def weight(array, start):
        whole = wholes[array]
        value = whole[:, :, :, :, :, pl.ds(start, 256)]
        return value.reshape(128 * whole.shape[4], 256)

    first = lengths_ref[0, 0]
    second = first + lengths_ref[0, 1]
    bounds = (first, second, second + lengths_ref[0, 2])
    melf[8:, :] = mel_ref[...].astype(F32)

    row_at = lax.broadcasted_iota(jnp.int32, (256, channels), 0)
    low_part, r = row_at // 128, row_at % 128
    at = (r >= SPAN).astype(jnp.int32) + (r >= 2 * SPAN).astype(jnp.int32)
    at = jnp.where(r >= 3 * SPAN, 3, at)
    column = r - SPAN * at
    spread = []
    for b in range(3):
        value = jnp.zeros((256, channels), F32)
        for a in range(3):
            w = w_first_ref[a, b : b + 1, :]
            top = w.astype(BF16).astype(F32)
            value = jnp.where(at == a, jnp.where(low_part == 0, top, w - top), value)
        spread.append(value)

    pl.semaphore_wait(barrier, len(greeted))
    edge_copy = pass_on(mel_ref.at[pl.ds(4 * tokens - 8, 8), :], edge, after, 0)
    edge_copy.start()
    gather.step(0, 1)
    gather.step(1, 1)
    for array in range(6):
        own_copy(array).wait()

    def make_band(f, carry):
        value = jnp.zeros((256, channels), F32)
        for b in range(3):
            value = jnp.where(column == 2 * f + b, spread[b], value)
        band[f] = value.astype(BF16)
        return carry

    lax.fori_loop(0, QUARTER, make_band, 0)
    frame_at = 4 * tokens * tm + 4 * lax.broadcasted_iota(jnp.int32, (tokens, bins), 0)
    seg_here = segments(frame_at, bounds, frames_all)

    def frame(d):
        return melf[pl.ds(8 + d, tokens, stride=4), :]

    def same(d):
        return (segments(frame_at + d, bounds, frames_all) == seg_here).astype(F32)

    bin_at = lax.broadcasted_iota(jnp.int32, (bins, 256), 0)
    place = lax.broadcasted_iota(jnp.int32, (bins, 256), 1)
    half, within = place // 128, place % 128

    def lay_out(v, frames):
        total = jnp.zeros((tokens, 256), F32)
        for a in range(3):
            taken = within - SPAN * a
            chosen = (taken >= 0) & (taken < SPAN) & (bin_at == 40 * half - 1 + taken)
            total = total + dot(frames[a].astype(BF16), chosen.astype(F32).astype(BF16))
        total = total.astype(BF16)
        for h in range(2):
            piece = total[:, 128 * h : 128 * (h + 1)]
            x_ref[h, v * tokens : (v + 1) * tokens, 0:128] = piece
            x_ref[h, v * tokens : (v + 1) * tokens, 128:256] = piece

    up2 = same(2)
    lay_out(2, (frame(1) * up2, frame(2) * up2, frame(3) * same(3)))
    edge_copy.wait_recv()
    melf[0:8, :] = edge[...].astype(F32)
    low2 = same(-2)
    lay_out(1, (frame(-1) * same(-1), frame(0), frame(1) * same(1)))
    lay_out(0, (frame(-3) * same(-3), frame(-2) * low2, frame(-1) * low2))

    def spill(pair, slot):
        return pltpu.make_async_copy(pairs.at[slot], spilled.at[pair], spill_sems.at[slot])

    def fetch(pair, slot):
        return pltpu.make_async_copy(spilled.at[pair], pairs.at[slot], fetch_sems.at[slot])

    def advance(at, steps):
        for number, todo in steps.items():

            @pl.when(at == number)
            def _():
                for phase, step in todo:
                    gather.step(phase, step)

    def first_step(pair, carry):
        advance(pair, FIRST_STEPS)
        h = pair // 10
        f = 2 * pair - 20 * h
        slot = pair % 3

        @pl.when(pair >= 3)
        def _():
            spill(pair - 3, slot).wait()

        for part in range(2):
            for v in range(3):
                made = dot(x_ref[h, v * tokens : (v + 1) * tokens, :], band[f + part])
                pairs[slot, part, :, v * channels : (v + 1) * channels] = jnp.maximum(made, 0.0).astype(BF16)
        spill(pair, slot).start()
        return carry

    lax.fori_loop(0, QUARTER, first_step, 0)
    for pair in range(QUARTER - 3, QUARTER):
        spill(pair, pair % 3).wait()
    fetch(0, 0).start()
    pairs[2, 1] = jnp.zeros(pairs.shape[2:], BF16)

    gather.step(0, 5)
    depth = ws.shape[4]

    def unpack(i, carry):
        group = w2.at[pl.ds(pl.multiple_of(8 * depth * i, 16), 8 * depth), :]
        for s in range(8):
            group[s * depth : (s + 1) * depth, :] = ws[i // 4, i % 4, s // 2, s % 2]
        return carry

    lax.fori_loop(0, 16, unpack, 0)
    for a in range(3):
        for b in range(3):
            start = (3 * a + b) * channels
            w2s[b, a * channels : (a + 1) * channels, :] = w2[start : start + channels, :]

    def second_step(pair, carry):
        advance(pair, SECOND_STEPS)
        slot = pair % 3
        fetch(pair, slot).wait()

        @pl.when(pair < QUARTER - 1)
        def _():
            fetch(pair + 1, (pair + 1) % 3).start()

        total = dot(pairs[(pair + 2) % 3, 1], w2s[0]) + dot(pairs[slot, 0], w2s[1]) + dot(pairs[slot, 1], w2s[2])
        columns = pl.ds(pl.multiple_of(pair * channels, channels), channels)
        sub[:, columns] = jnp.maximum(total, 0.0).astype(BF16)
        return carry

    lax.fori_loop(0, QUARTER, second_step, 0)
    gather.step(1, 7)

    def project(start):
        columns = pl.ds(start, 256)
        hidden[:, columns] = dot(sub[...], weight(1, start))

    over_columns(2, project)
    gather.step(3, 5)
    gather.step(2, 6)
    over_columns(4, project, 2)
    norm_rows(hidden, gain_attn_ref, normed)
    gather.step(2, 7)

    def mix_keyval(start):
        keyval[WINDOW : WINDOW + tokens, pl.ds(start, 256)] = dot(
            normed[...], weight(2, WIDTH + start)
        ).astype(BF16)

    over_columns(2 * WIDTH // 256, mix_keyval)
    halos = (
        pass_on(keyval.at[pl.ds(tokens, WINDOW), :], keyval.at[pl.ds(0, WINDOW), :], after, 1),
        pass_on(
            keyval.at[pl.ds(WINDOW, WINDOW), :], keyval.at[pl.ds(WINDOW + tokens, WINDOW), :], before, 2
        ),
    )
    for copy in halos:
        copy.start()
    gather.step(3, 6)

    def mix_query(start):
        query[:, pl.ds(start, 256)] = dot(normed[...], weight(2, start)).astype(BF16)

    over_columns(WIDTH // 256, mix_query)

    base = tokens * tm
    reach = 3 * WINDOW
    q_at = lax.broadcasted_iota(jnp.int32, (WINDOW, 1), 0)
    k_at = lax.broadcasted_iota(jnp.int32, (1, reach), 1) - WINDOW
    near = jnp.abs(k_at - q_at) <= WINDOW
    blocks = tokens // WINDOW

    def attend(i, carry):
        block = (i + 1) % blocks

        @pl.when(i == blocks - 2)
        def _():
            for copy in halos:
                copy.wait_recv()

        start = pl.multiple_of(block * WINDOW, WINDOW)
        q_rows, k_rows = pl.ds(start, WINDOW), pl.ds(start, reach)
        q_seg = segments(4 * (base + start + q_at), bounds, frames_all)
        k_seg = segments(4 * (base + start + k_at), bounds, frames_all)
        bias[...] = jnp.where(near & (q_seg == k_seg), 0.0, -1e30)
        for head in range(HEADS):
            own = slice(head * HEAD_DIM, (head + 1) * HEAD_DIM)
            values = slice(WIDTH + head * HEAD_DIM, WIDTH + (head + 1) * HEAD_DIM)
            scores = lax.dot_general(
                query[q_rows, own], keyval[k_rows, own], (((1,), (1,)), ((), ())),
                preferred_element_type=F32,
            ) * HEAD_DIM ** (-0.5) + bias[...]
            exped = jnp.exp(scores - jnp.max(scores, axis=-1, keepdims=True))
            share = 1.0 / jnp.sum(exped, axis=-1, keepdims=True)
            context[q_rows, own] = dot((exped * share).astype(BF16), keyval[k_rows, values]).astype(BF16)
        return carry

    lax.fori_loop(0, blocks, attend, 0)

    gather.step(3, 7)

    def attend_out(start):
        columns = pl.ds(start, 256)
        hidden[:, columns] = hidden[:, columns] + dot(context[...], weight(3, start))

    over_columns(WIDTH // 256, attend_out)
    norm_rows(hidden, gain_conv_ref, normed)

    def gate(start):
        value = dot(normed[...], weight(4, start))
        opening = dot(normed[...], weight(4, WIDTH + start))
        gated = (value * jax.nn.sigmoid(opening)).astype(BF16)
        extended[8 : 8 + tokens, pl.ds(start, 256)] = gated.astype(F32)

    over_columns(WIDTH // 256, gate)
    edges = (
        pass_on(extended.at[pl.ds(tokens, 8), :], extended.at[pl.ds(0, 8), :], after, 3),
        pass_on(extended.at[pl.ds(8, 8), :], extended.at[pl.ds(8 + tokens, 8), :], before, 4),
    )
    for copy in edges:
        copy.start()
    rows_at_once = 64
    groups = tokens // rows_at_once
    reach = KERNEL // 2

    def depth_step(i, carry):
        group = (i + 1) % groups

        @pl.when(i == groups - 2)
        def _():
            for copy in edges:
                copy.wait_recv()

        start = pl.multiple_of(group * rows_at_once, rows_at_once)
        position = base + start + lax.broadcasted_iota(jnp.int32, (rows_at_once, 1), 0)
        own = segments(4 * position, bounds, frames_all)
        kept = [
            (segments(4 * (position + k - reach), bounds, frames_all) == own).astype(F32)
            for k in range(KERNEL)
        ]
        for n in range(WIDTH // 256):
            columns = slice(n * 256, (n + 1) * 256)
            window = extended[pl.ds(start, rows_at_once + 16), columns]
            total = jnp.zeros((rows_at_once, 256), F32)
            for k in range(KERNEL):
                taken = window[4 + k : 4 + k + rows_at_once]
                total = total + taken * w_depth_ref[k : k + 1, columns] * kept[k]
            context[pl.ds(start, rows_at_once), columns] = (total * jax.nn.sigmoid(total)).astype(BF16)
        return carry

    lax.fori_loop(0, groups, depth_step, 0)

    def point_out(start):
        columns = pl.ds(start, 256)
        hidden[:, columns] = hidden[:, columns] + dot(context[...], weight(5, start))

    over_columns(WIDTH // 256, point_out)
    norm_rows(hidden, gain_out_ref, out_ref)
    gather.finish()
    for copy in (edge_copy,) + halos + edges:
        copy.wait_send()


def on_device(
    mel_frames, lengths, w_first, w_second, w_proj, gain_attn, w_qkv, w_out, gain_conv,
    w_point_in, w_depth, w_point_out, gain_out,
):
    mel = mel_frames[0]
    tokens = mel.shape[0] // 4
    bins = mel.shape[1]
    channels = w_first.shape[-1]
    shards = (w_second, w_proj, w_qkv, w_out, w_point_in, w_point_out)
    vmem = pl.BlockSpec(memory_space=pltpu.VMEM)
    hbm = pl.BlockSpec(memory_space=pl.ANY)
    encoded, _ = pl.pallas_call(
        block_kernel,
        out_shape=[
            jax.ShapeDtypeStruct((tokens, WIDTH), BF16),
            jax.ShapeDtypeStruct((QUARTER, 2, tokens, 3 * channels), BF16),
        ],
        in_specs=[pl.BlockSpec(memory_space=pltpu.SMEM)] + [vmem] * 6 + [hbm] * 6,
        out_specs=[vmem, hbm],
        scratch_shapes=[
            pltpu.VMEM((8, bins), BF16),
            pltpu.VMEM((4 * tokens + 8, bins), F32),
            pltpu.VMEM((2, 3 * tokens, 256), BF16),
            pltpu.VMEM((QUARTER, 256, channels), BF16),
            *[pltpu.VMEM((4, 4, 4, 2) + s.shape, BF16) for s in shards],
            pltpu.VMEM((9 * channels, channels), BF16),
            pltpu.VMEM((3, 3 * channels, channels), BF16),
            pltpu.VMEM((3, 2, tokens, 3 * channels), BF16),
            pltpu.VMEM((tokens, QUARTER * channels), BF16),
            pltpu.VMEM((tokens, WIDTH), F32),
            pltpu.VMEM((tokens, WIDTH), BF16),
            pltpu.VMEM((tokens, WIDTH), BF16),
            pltpu.VMEM((tokens + 2 * WINDOW, 2 * WIDTH), BF16),
            pltpu.VMEM((WINDOW, 3 * WINDOW), F32),
            pltpu.VMEM((tokens, WIDTH), BF16),
            pltpu.VMEM((tokens + 16, WIDTH), F32),
            pltpu.SemaphoreType.DMA((len(CHUNKS), SLOTS)),
            pltpu.SemaphoreType.DMA((len(CHUNKS), SLOTS)),
            pltpu.SemaphoreType.DMA((6,)),
            pltpu.SemaphoreType.DMA((5,)),
            pltpu.SemaphoreType.DMA((5,)),
            pltpu.SemaphoreType.DMA((3,)),
            pltpu.SemaphoreType.DMA((3,)),
        ],
        compiler_params=pltpu.CompilerParams(
            collective_id=0, has_side_effects=True, vmem_limit_bytes=VMEM_LIMIT
        ),
    )(
        lengths, mel, w_first, gain_attn[None], gain_conv[None], w_depth, gain_out[None], *shards
    )
    return encoded[None]


def solution(mesh):
    weight = P(("rec", "tm"), None)
    placed = (
        P("rec", "tm", None), P("rec", None), P(), weight, weight, P(), weight, weight, P(),
        weight, P(), weight, P(),
    )
    return jax.shard_map(
        on_device, mesh=mesh, in_specs=placed, out_specs=P("rec", "tm", None), check_vma=False
    )
```

```python
import jax
import jax.numpy as jnp
from jax import lax
from jax.experimental import pallas as pl
from jax.experimental.pallas import tpu as pltpu
from jax.sharding import PartitionSpec as P

WIDTH = 1024
HEADS = 8
KERNEL = 9
WINDOW = 128
HEAD_DIM = 128
QUARTER = 20
KEPT = 6
LEAD = 16
SPAN = 41
NORM_EPSILON = 1e-05
VMEM_LIMIT = 63 * 2**20
BF16 = jnp.bfloat16
F32 = jnp.float32
MESH = pl.DeviceIdType.MESH

ORDERS = (("x", "y", "z"), ("y", "z", "x"), ("z", "x", "y"))
PLACES = ((0, 0), (1, 0), (2, 0), (3, 0), (3, WIDTH), (3, 3 * WIDTH))
CHUNKS = (
    (0, 0, 128, 0), (0, 128, 128, 1),
    (1, 0, 256, 0), (1, 256, 384, 1), (1, 640, 384, 2),
    (2, 0, 1024, 0), (2, 1024, 1024, 1), (2, 2048, 1024, 2),
    (3, 0, 1408, 0), (3, 1408, 1280, 1), (3, 2688, 1408, 2),
)
PHASES = ((0, 1), (2, 3, 4), (5, 6, 7), (8, 9, 10))
DIRECT = (
    ((), (0, 1, 2)), ((0, 1, 2), (3, 4, 5)), ((3, 4, 5), (6, 7, 8, 9)), ((6, 7, 8), (10, 11, 12)),
    ((9, 10, 11, 12), ()),
)
FORWARDED = (
    ((), (0, 1, 2)), ((0, 1, 2), (3, 4, 5)), ((3, 4, 5), (6, 7, 10)), ((6, 7), (8, 9, 11, 12)),
    ((8, 9), (13,)), ((10, 11, 12, 13), ()),
)
FIRST_STEPS = {0: ((0, 2),), 2: ((1, 2),), 3: ((2, 1),), 9: ((0, 3),), 11: ((2, 2),), 12: ((3, 1),), 15: ((1, 3),), 18: ((0, 4),), 19: ((2, 3), (3, 2))}
SECOND_STEPS = {9: ((1, 4),), 14: ((2, 4),), 15: ((3, 3),), 19: ((1, 5),)}
PROJECT_STEPS = {2: ((2, 5),)}
KEYVAL_STEPS = {0: ((3, 4),)}
QUERY_STEPS = {3: ((3, 5),)}
ATTEND_STEPS = {}
SLOTS = 14


def dot(a, b):
    return jnp.dot(a, b, preferred_element_type=F32)


def segments(positions, bounds, limit):
    counted = sum((positions >= b).astype(jnp.int32) for b in bounds)
    return jnp.where((positions >= 0) & (positions < limit), counted, -1)


def normalised(values, gain):
    centred = values - jnp.mean(values, axis=-1, keepdims=True)
    variance = jnp.mean(centred * centred, axis=-1, keepdims=True)
    return centred * lax.rsqrt(variance + NORM_EPSILON) * gain


def norm_rows(source, gain_ref, target, step=64):
    gain = gain_ref[...]

    def body(i, carry):
        rows = pl.ds(pl.multiple_of(i * step, step), step)
        target[rows, :] = normalised(source[rows, :], gain).astype(target.dtype)
        return carry

    lax.fori_loop(0, source.shape[0] // step, body, 0)


def over_columns(count, body, before=lambda n: None):
    def step(n, carry):
        before(n)
        body(pl.multiple_of(n * 256, 256))
        return carry

    lax.fori_loop(0, count, step, 0)


class Gather:
    def __init__(self, shards, wholes, send_sems, recv_sems):
        self.shards, self.wholes = shards, wholes
        self.send_sems, self.recv_sems = send_sems, recv_sems
        tm = lax.axis_index("tm")
        self.here = {"z": lax.axis_index("rec"), "x": tm // 8, "y": (tm // 2) % 4}
        self.core = tm % 2
        self.near = {
            (axis, step): {**self.here, axis: (self.here[axis] + step) % 4}
            for axis in ("x", "y", "z")
            for step in (1, 2, 3)
        }

    def device(self, position, core):
        return {"rec": position["z"], "tm": position["x"] * 8 + position["y"] * 2 + core}

    def peers(self):
        chips = [self.device(position, self.core) for position in self.near.values()]
        return chips + [self.device(self.here, 1 - self.core)]

    def view(self, chunk, stage, position, half=None):
        array, column, columns, order = CHUNKS[chunk]
        free = ORDERS[order][: stage - 1]
        index = []
        for axis in ("z", "x", "y"):
            if axis not in free:
                index.append(position[axis])
            elif half is not None and axis == free[0]:
                index.append(pl.ds(2 * half, 2))
            else:
                index.append(slice(None))
        return self.wholes[array].at[tuple(index) + (self.core, slice(None), pl.ds(column, columns))]

    def copy(self, chunk, slot):
        array, column, columns, order = CHUNKS[chunk]
        axes = ORDERS[order]
        target = None
        direct = chunk in PHASES[0]
        siblings = 9 if direct else 10
        if slot < 3:
            target = self.near[axes[0], (1, 3, 2)[slot]]
            place = self.view(chunk, 1, self.here)
            source = place if array == 3 else self.shards[array].at[:, pl.ds(column, columns)]
        elif slot < 6 or (direct and slot < 9):
            stage = 2 if slot < 6 else 3
            target = self.near[axes[stage - 1], (1, 3, 2)[slot % 3]]
            source = self.view(chunk, stage, self.here)
            place = source
        elif slot < siblings:
            at = slot - 6
            target = self.near[axes[2], (1, 3, 1, 3)[at]]
            if at < 2:
                source = self.view(chunk, 3, self.here)
            else:
                source = self.view(chunk, 3, self.near[axes[2], (3, 1)[at - 2]], at - 2)
            place = source
        else:
            axis = axes[2]
            at = slot - siblings
            source = self.view(chunk, 3, self.here if at == 0 else self.near[axis, (3, 1, 2)[at - 1]])
            place = source
        where = self.device(self.here, 1 - self.core) if target is None else self.device(target, self.core)
        return pltpu.make_async_remote_copy(
            src_ref=source, dst_ref=place, send_sem=self.send_sems.at[chunk, slot],
            recv_sem=self.recv_sems.at[chunk, slot], device_id=where, device_id_type=MESH,
        )

    def step(self, phase, number):
        awaited, started = (DIRECT if phase == 0 else FORWARDED)[number - 1]
        for chunk in PHASES[phase]:
            for slot in awaited:
                self.copy(chunk, slot).wait_recv()
            for slot in started:
                self.copy(chunk, slot).start()

    def finish(self):
        for chunk in range(len(CHUNKS)):
            for slot in range(13 if chunk in PHASES[0] else SLOTS):
                self.copy(chunk, slot).wait_send()


def block_kernel(
    lengths_ref, mel_ref, w_first_ref, gain_attn_ref, gain_conv_ref, w_depth_ref, gain_out_ref,
    ws_shard, wp_shard, wq_shard, wo_shard, wi_shard, wu_shard,
    out_ref, spilled,
    edge, melf, x_ref, band, ws, wp, wq, wr, w2, frames_made, carried, sub,
    hidden, normed, query, keyval, bias, context, extended,
    send_sems, recv_sems, own_sems, halo_send, halo_recv, spill_sems, fetch_sems,
):
    tokens = mel_ref.shape[0] // 4
    channels = w_first_ref.shape[-1]
    bins = mel_ref.shape[1]
    tm = lax.axis_index("tm")
    count = lax.axis_size("tm")
    rec = lax.axis_index("rec")
    frames_all = mel_ref.shape[0] * count
    shards = (ws_shard, wp_shard, wq_shard, wo_shard, wi_shard, wu_shard)
    wholes = (ws, wp, wq, wr)
    gather = Gather(shards, wholes, send_sems, recv_sems)
    after = {"rec": rec, "tm": (tm + 1) % count}
    before = {"rec": rec, "tm": (tm + count - 1) % count}

    barrier = pltpu.get_barrier_semaphore()
    greeted = gather.peers() + [after, before]
    for device in greeted:
        pl.semaphore_signal(barrier, inc=1, device_id=device, device_id_type=MESH)

    def own_copy(array):
        here = gather.here
        whole, column = PLACES[array]
        width = pl.ds(column, shards[array].shape[1])
        place = wholes[whole].at[here["z"], here["x"], here["y"], gather.core, slice(None), width]
        return pltpu.make_async_copy(shards[array], place, own_sems.at[array])

    for array in range(6):
        own_copy(array).start()

    def pass_on(source, place, device, number):
        return pltpu.make_async_remote_copy(
            src_ref=source, dst_ref=place, send_sem=halo_send.at[number],
            recv_sem=halo_recv.at[number], device_id=device, device_id_type=MESH,
        )

    def weight(array, start):
        whole, column = PLACES[array]
        whole = wholes[whole]
        start = pl.multiple_of(start + column, 128)
        value = whole[:, :, :, :, :, pl.ds(start, 256)]
        return value.reshape(128 * whole.shape[4], 256)

    first = lengths_ref[0, 0]
    second = first + lengths_ref[0, 1]
    bounds = (first, second, second + lengths_ref[0, 2])
    melf[0 : 4 * LEAD, :] = jnp.zeros((4 * LEAD, bins), F32)
    melf[4 * LEAD :, :] = mel_ref[...].astype(F32)

    row_at = lax.broadcasted_iota(jnp.int32, (256, channels), 0)
    low_part, r = row_at // 128, row_at % 128
    at = (r >= SPAN).astype(jnp.int32) + (r >= 2 * SPAN).astype(jnp.int32)
    at = jnp.where(r >= 3 * SPAN, 3, at)
    column = r - SPAN * at
    spread = []
    for b in range(3):
        value = jnp.zeros((256, channels), F32)
        for a in range(3):
            w = w_first_ref[a, b : b + 1, :]
            top = w.astype(BF16).astype(F32)
            value = jnp.where(at == a, jnp.where(low_part == 0, top, w - top), value)
        spread.append(value)

    pl.semaphore_wait(barrier, len(greeted))
    edge_copy = pass_on(mel_ref.at[pl.ds(4 * tokens - 8, 8), :], edge, after, 0)
    edge_copy.start()
    gather.step(0, 1)
    gather.step(1, 1)
    for array in range(6):
        own_copy(array).wait()

    def make_band(f, carry):
        value = jnp.zeros((256, channels), F32)
        for b in range(3):
            value = jnp.where(column == 2 * f + b, spread[b], value)
        band[f] = value.astype(BF16)
        return carry

    lax.fori_loop(0, QUARTER, make_band, 0)
    token_at = tokens * tm + lax.broadcasted_iota(jnp.int32, (tokens, 128), 0)
    seg_here = segments(4 * token_at, bounds, frames_all)
    for k, d in ((0, -2), (1, 2)):
        carried[k] = (segments(4 * token_at + d, bounds, frames_all) == seg_here).astype(F32)

    def laid_out(first_token, count, centre):
        at = 4 * (tokens * tm + first_token + lax.broadcasted_iota(jnp.int32, (count, bins), 0)) + centre
        own = segments(at, bounds, frames_all)
        total = jnp.zeros((count, 256), F32)
        for a in range(3):
            start = 4 * (LEAD + first_token) + centre + a - 1
            taken = melf[pl.ds(start, count, stride=4), :]
            if a != 1:
                taken = taken * (segments(at + a - 1, bounds, frames_all) == own).astype(F32)
            column = within - SPAN * a
            chosen = (column >= 0) & (column < SPAN) & (bin_at == 40 * half - 1 + column)
            total = total + dot(taken.astype(BF16), chosen.astype(F32).astype(BF16))
        return total.astype(BF16)

    def lay_out(row, first_token, count, centre):
        total = laid_out(first_token, count, centre)
        for h in range(2):
            piece = total[:, 128 * h : 128 * (h + 1)]
            x_ref[h, row : row + count, 0:128] = piece
            x_ref[h, row : row + count, 128:256] = piece

    bin_at = lax.broadcasted_iota(jnp.int32, (bins, 256), 0)
    place = lax.broadcasted_iota(jnp.int32, (bins, 256), 1)
    half, within = place // 128, place % 128

    lay_out(LEAD, 0, tokens, 2)
    edge_copy.wait_recv()
    melf[4 * LEAD - 8 : 4 * LEAD, :] = edge[...].astype(F32)
    lay_out(LEAD + tokens, 0, tokens, 0)
    lay_out(0, -LEAD, LEAD, 2)

    def spill(pair, slot):
        source = frames_made.at[pl.ds(2 * slot, 2)]
        return pltpu.make_async_copy(source, spilled.at[pair - KEPT - 3], spill_sems.at[slot - KEPT])

    def slot_of(pair):
        turn = pair % (KEPT + 3)
        return jnp.where(turn < KEPT, turn, KEPT + (QUARTER - 1 - turn) % 3)

    def fetch(pair):
        number = pair - KEPT - 3
        place = frames_made.at[pl.ds(2 * slot_of(pair), 2)]
        return pltpu.make_async_copy(spilled.at[number], place, fetch_sems.at[number])

    def advance(at, steps):
        for number, todo in steps.items():

            @pl.when(at == number)
            def _():
                for phase, step in todo:
                    gather.step(phase, step)

    def first_step(job, carry):
        advance(job, FIRST_STEPS)
        stays = (job < 2 * KEPT) & (job % 2 == 1)
        turn = jnp.where(job < 2 * KEPT, job // 2, job - KEPT)
        pair = jnp.where(stays, turn, QUARTER - 1 - turn)
        slot = jnp.where(stays, turn, KEPT + turn % 3)

        @pl.when(jnp.logical_not(stays) & (turn >= 3))
        def _():
            spill(pair + 3, slot).wait()

        h = pair // 10
        f = 2 * pair - 20 * h
        for part in range(2):
            made = dot(x_ref[h], band[f + part])
            frames_made[2 * slot + part] = jnp.maximum(made, 0.0).astype(BF16)

        @pl.when(jnp.logical_not(stays) & (pair >= KEPT + 3))
        def _():
            spill(pair, slot).start()

        return carry

    lax.fori_loop(0, QUARTER, first_step, 0)
    nothing = 2 * (KEPT + 3)
    frames_made[nothing] = jnp.zeros(frames_made.shape[1:], BF16)

    gather.step(0, 5)
    depth = ws.shape[4]

    def unpack(i, carry):
        group = w2.at[pl.ds(pl.multiple_of(8 * depth * i, 16), 8 * depth), :]
        for s in range(8):
            group[s * depth : (s + 1) * depth, :] = ws[i // 4, i % 4, s // 2, s % 2]
        return carry

    lax.fori_loop(0, 16, unpack, 0)
    def second_step(pair, carry):
        advance(pair, SECOND_STEPS)

        @pl.when((pair >= 2) & (pair < QUARTER - KEPT - 1))
        def _():
            fetch(pair + KEPT + 1).start()

        @pl.when(pair >= KEPT + 3)
        def _():
            fetch(pair).wait()

        last = jnp.where(pair == 0, nothing, 2 * slot_of(pair - 1) + 1)
        used = (last, 2 * slot_of(pair), 2 * slot_of(pair) + 1)

        def taps(a, first_row, rows):
            total = None
            for b in range(3):
                start = (3 * a + b) * channels
                made = dot(frames_made[used[b], first_row : first_row + rows, :], w2[start : start + channels, :])
                total = made if total is None else total + made
            return total

        below = taps(0, 0, LEAD + tokens)[LEAD - 1 : LEAD - 1 + tokens]
        centre = taps(1, LEAD + tokens, tokens)
        above = taps(2, LEAD, tokens)
        for part in range(channels // 128):
            lanes = slice(part * 128, (part + 1) * 128)
            total = centre[:, lanes] + below[:, lanes] * carried[0] + above[:, lanes] * carried[1]
            columns = pl.ds(pl.multiple_of(pair * channels + part * 128, 128), 128)
            sub[:, columns] = jnp.maximum(total, 0.0).astype(BF16)
        return carry

    lax.fori_loop(0, QUARTER, second_step, 0)
    gather.step(1, 6)

    def project(start):
        columns = pl.ds(start, 256)
        hidden[:, columns] = dot(sub[...], weight(1, start))

    over_columns(WIDTH // 256, project, lambda n: advance(n, PROJECT_STEPS))
    norm_rows(hidden, gain_attn_ref, normed)
    gather.step(2, 6)

    def mix_keyval(start):
        keyval[WINDOW : WINDOW + tokens, pl.ds(start, 256)] = dot(
            normed[...], weight(2, WIDTH + start)
        ).astype(BF16)

    over_columns(2 * WIDTH // 256, mix_keyval, lambda n: advance(n, KEYVAL_STEPS))
    halos = (
        pass_on(keyval.at[pl.ds(tokens, WINDOW), :], keyval.at[pl.ds(0, WINDOW), :], after, 1),
        pass_on(
            keyval.at[pl.ds(WINDOW, WINDOW), :], keyval.at[pl.ds(WINDOW + tokens, WINDOW), :], before, 2
        ),
    )
    for copy in halos:
        copy.start()

    def mix_query(start):
        query[:, pl.ds(start, 256)] = dot(normed[...], weight(2, start)).astype(BF16)

    over_columns(WIDTH // 256, mix_query, lambda n: advance(n, QUERY_STEPS))

    base = tokens * tm
    reach = 3 * WINDOW
    q_at = lax.broadcasted_iota(jnp.int32, (WINDOW, 1), 0)
    k_at = lax.broadcasted_iota(jnp.int32, (1, reach), 1) - WINDOW
    near = jnp.abs(k_at - q_at) <= WINDOW
    blocks = tokens // WINDOW

    def attend(i, carry):
        block = (i + 1) % blocks
        advance(i, ATTEND_STEPS)

        @pl.when(i == blocks - 2)
        def _():
            for copy in halos:
                copy.wait_recv()

        start = pl.multiple_of(block * WINDOW, WINDOW)
        q_rows, k_rows = pl.ds(start, WINDOW), pl.ds(start, reach)
        q_seg = segments(4 * (base + start + q_at), bounds, frames_all)
        k_seg = segments(4 * (base + start + k_at), bounds, frames_all)
        bias[...] = jnp.where(near & (q_seg == k_seg), 0.0, -1e30)
        lanes = [slice(head * HEAD_DIM, (head + 1) * HEAD_DIM) for head in range(HEADS)]
        masked = bias[...]
        scores = [
            lax.dot_general(
                query[q_rows, own], keyval[k_rows, own], (((1,), (1,)), ((), ())),
                preferred_element_type=F32,
            ) * HEAD_DIM ** (-0.5) + masked
            for own in lanes
        ]
        tops = [jnp.max(score, axis=-1, keepdims=True) for score in scores]
        exped = [jnp.exp(score - top) for score, top in zip(scores, tops)]
        shares = [1.0 / jnp.sum(e, axis=-1, keepdims=True) for e in exped]
        for head, own in enumerate(lanes):
            values = slice(WIDTH + head * HEAD_DIM, WIDTH + (head + 1) * HEAD_DIM)
            probabilities = (exped[head] * shares[head]).astype(BF16)
            context[q_rows, own] = dot(probabilities, keyval[k_rows, values]).astype(BF16)
        return carry

    lax.fori_loop(0, blocks, attend, 0)

    gather.step(3, 6)

    def attend_out(start):
        columns = pl.ds(start, 256)
        hidden[:, columns] = hidden[:, columns] + dot(context[...], weight(3, start))

    over_columns(WIDTH // 256, attend_out)
    norm_rows(hidden, gain_conv_ref, normed)

    def gate(start):
        value = dot(normed[...], weight(4, start))
        opening = dot(normed[...], weight(4, WIDTH + start))
        gated = (value * jax.nn.sigmoid(opening)).astype(BF16)
        extended[8 : 8 + tokens, pl.ds(start, 256)] = gated.astype(F32)

    over_columns(WIDTH // 256, gate)
    edges = (
        pass_on(extended.at[pl.ds(tokens, 8), :], extended.at[pl.ds(0, 8), :], after, 3),
        pass_on(extended.at[pl.ds(8, 8), :], extended.at[pl.ds(8 + tokens, 8), :], before, 4),
    )
    for copy in edges:
        copy.start()
    rows_at_once = 64
    groups = tokens // rows_at_once
    reach = KERNEL // 2

    def depth_step(i, carry):
        group = (i + 1) % groups

        @pl.when(i == groups - 2)
        def _():
            for copy in edges:
                copy.wait_recv()

        start = pl.multiple_of(group * rows_at_once, rows_at_once)
        position = base + start + lax.broadcasted_iota(jnp.int32, (rows_at_once, 1), 0)
        own = segments(4 * position, bounds, frames_all)
        kept = [
            (segments(4 * (position + k - reach), bounds, frames_all) == own).astype(F32)
            for k in range(KERNEL)
        ]
        for n in range(WIDTH // 256):
            columns = slice(n * 256, (n + 1) * 256)
            window = extended[pl.ds(start, rows_at_once + 16), columns]
            total = jnp.zeros((rows_at_once, 256), F32)
            for k in range(KERNEL):
                taken = window[4 + k : 4 + k + rows_at_once]
                total = total + taken * w_depth_ref[k : k + 1, columns] * kept[k]
            context[pl.ds(start, rows_at_once), columns] = (total * jax.nn.sigmoid(total)).astype(BF16)
        return carry

    lax.fori_loop(0, groups, depth_step, 0)

    def point_out(start):
        columns = pl.ds(start, 256)
        hidden[:, columns] = hidden[:, columns] + dot(context[...], weight(5, start))

    over_columns(WIDTH // 256, point_out)
    norm_rows(hidden, gain_out_ref, out_ref)
    gather.finish()
    for copy in (edge_copy,) + halos + edges:
        copy.wait_send()


def on_device(
    mel_frames, lengths, w_first, w_second, w_proj, gain_attn, w_qkv, w_out, gain_conv,
    w_point_in, w_depth, w_point_out, gain_out,
):
    mel = mel_frames[0]
    tokens = mel.shape[0] // 4
    bins = mel.shape[1]
    channels = w_first.shape[-1]
    shards = (w_second, w_proj, w_qkv, w_out, w_point_in, w_point_out)
    vmem = pl.BlockSpec(memory_space=pltpu.VMEM)
    hbm = pl.BlockSpec(memory_space=pl.ANY)
    encoded, _ = pl.pallas_call(
        block_kernel,
        out_shape=[
            jax.ShapeDtypeStruct((tokens, WIDTH), BF16),
            jax.ShapeDtypeStruct((QUARTER - KEPT - 3, 2, LEAD + 2 * tokens, channels), BF16),
        ],
        in_specs=[pl.BlockSpec(memory_space=pltpu.SMEM)] + [vmem] * 6 + [hbm] * 6,
        out_specs=[vmem, hbm],
        scratch_shapes=[
            pltpu.VMEM((8, bins), BF16),
            pltpu.VMEM((4 * (LEAD + tokens), bins), F32),
            pltpu.VMEM((2, LEAD + 2 * tokens, 256), BF16),
            pltpu.VMEM((QUARTER, 256, channels), BF16),
            *[pltpu.VMEM((4, 4, 4, 2) + s.shape, BF16) for s in shards[:3]],
            pltpu.VMEM((4, 4, 4, 2, w_out.shape[0], 4 * WIDTH), BF16),
            pltpu.VMEM((9 * channels, channels), BF16),
            pltpu.VMEM((2 * (KEPT + 3) + 1, LEAD + 2 * tokens, channels), BF16),
            pltpu.VMEM((2, tokens, 128), F32),
            pltpu.VMEM((tokens, QUARTER * channels), BF16),
            pltpu.VMEM((tokens, WIDTH), F32),
            pltpu.VMEM((tokens, WIDTH), BF16),
            pltpu.VMEM((tokens, WIDTH), BF16),
            pltpu.VMEM((tokens + 2 * WINDOW, 2 * WIDTH), BF16),
            pltpu.VMEM((WINDOW, 3 * WINDOW), F32),
            pltpu.VMEM((tokens, WIDTH), BF16),
            pltpu.VMEM((tokens + 16, WIDTH), F32),
            pltpu.SemaphoreType.DMA((len(CHUNKS), SLOTS)),
            pltpu.SemaphoreType.DMA((len(CHUNKS), SLOTS)),
            pltpu.SemaphoreType.DMA((6,)),
            pltpu.SemaphoreType.DMA((5,)),
            pltpu.SemaphoreType.DMA((5,)),
            pltpu.SemaphoreType.DMA((3,)),
            pltpu.SemaphoreType.DMA((QUARTER - KEPT - 3,)),
        ],
        compiler_params=pltpu.CompilerParams(
            collective_id=0, has_side_effects=True, vmem_limit_bytes=VMEM_LIMIT
        ),
    )(
        lengths, mel, w_first, gain_attn[None], gain_conv[None], w_depth, gain_out[None], *shards
    )
    return encoded[None]


def solution(mesh):
    weight = P(("rec", "tm"), None)
    placed = (
        P("rec", "tm", None), P("rec", None), P(), weight, weight, P(), weight, weight, P(),
        weight, P(), weight, P(),
    )
    return jax.shard_map(
        on_device, mesh=mesh, in_specs=placed, out_specs=P("rec", "tm", None), check_vma=False
    )
```
